32 devices in a mesh: filt: 16 (over z, y, x), depth: 2 (over core).
Axes of the slice: x: 2, y: 2, z: 4, core: 2. Of those that a mesh axis runs over, the one named last changes fastest.
Arguments:
- volume: bfloat16 [256, 8, 64, 128], P(None, 'depth', 'filt'), may hold values from -6 to 6
- weights: bfloat16 [128, 27, 256], P('filt'), may hold values from -0.078125 to 0.078125
- bias: float32 [128], replicated, may hold values from -3 to 3
- grad_out: bfloat16 [128, 8, 64, 128], P(None, 'depth', 'filt'), may hold values from -0.0234375 to 0.0234375
Outputs:
- output: bfloat16 [128, 8, 64, 128], P(None, 'depth', 'filt')
- grad_w: float32 [128, 27, 256], P('filt')
The draws below stay inside these ranges and needn't reach their ends.
All inputs are finite; a program needn't handle non-finite values.
Results may differ from the reference program's by a relative error of at most 0.001.
Values may be sent and summed in bfloat16 or wider, within the bound.
A program may use at most 64 MiB of HBM per device.

```python
import jax
import jax.numpy as jnp
from jax import lax

CIN = 256
COUT = 128
Y = 128
NZ = 8
X = 64


def spiked(array, own_key, source, target, shards_of, factor):
    owner, partner = [(jnp.arange(array.shape[axis_at]) // (array.shape[axis_at] // shards_of)).reshape([-1 if axis == axis_at else 1 for axis in range(array.ndim)]) for axis_at in (source, target)]
    chosen = jax.random.permutation(own_key, shards_of)[partner]
    strong = (owner == chosen) | (owner == (partner + shards_of // 2) % shards_of)
    return jnp.where(strong, factor * array, array)


def levels(stream_key, dims, shards, smallest, largest):
    gain, own = 1.0, jax.random.fold_in(stream_key, 6)
    for dim, parts in shards:
        draws = jnp.exp(jax.random.uniform(jax.random.fold_in(own, dim), (parts,), jnp.float32, smallest / len(shards), largest / len(shards)))
        gain = gain * jnp.repeat(draws, dims[dim] // parts).reshape([-1 if axis == dim else 1 for axis in range(len(dims))])
    return gain


def centred(own_key, dims, deviation, reach, shards=(), dtype=jnp.bfloat16):
    loudness = levels(own_key, dims, shards, -0.22, 0.18) if shards else 1.0
    drawn = jax.random.normal(own_key, dims, jnp.float32) * deviation * loudness
    return jnp.minimum(jnp.maximum(drawn, -reach), reach).astype(dtype)


def bell_draw_with(stream_key, shape, width, most, shards, heavy, held_as=jnp.bfloat16):
    drawn = width * jax.random.normal(stream_key, shape, jnp.float32)
    if shards:
        drawn = drawn * levels(stream_key, shape, shards, -0.22, 0.18)
    return jnp.clip(spiked(drawn, jax.random.fold_in(stream_key, 3), *heavy), -most, most).astype(held_as)


def setup_inputs(seed: int = 0) -> dict:
    key_of = jax.random.split(jax.random.key(seed), 5)
    return {
        "volume": centred(key_of[0], (CIN, NZ, X, Y), 1.0, 6.0, ((1, 2), (2, 16))),
        "weights": centred(key_of[1], (COUT, 27, CIN), (27 * CIN) ** -0.5, 0.078125, ((0, 16),)),
        "bias": centred(key_of[2], (COUT,), 0.5, 3.0, (), jnp.float32),
        "grad_out": bell_draw_with(key_of[3], (COUT, NZ, X, Y), (1.0 / (X * Y * NZ) ** 0.5), 0.0234375, ((1, 2), (2, 16)), (2, 0, 16, 2.0)),
    }


def reference(volume, weights, bias, grad_out):
    field = volume.astype(jnp.float32)
    kernel = weights.astype(jnp.float32).reshape(COUT, 3, 3, 3, CIN)
    forward = lax.conv_general_dilated(field[None], kernel, (1, 1, 1), ((1, 1), (1, 1), (1, 1)), dimension_numbers=("NCDHW", "ODHWI", "NCDHW"), precision=lax.Precision.HIGHEST)
    output = (forward[0] + bias[:, None, None, None]).astype(jnp.bfloat16)
    padded = jnp.pad(field, ((0, 0), (1, 1), (1, 1), (1, 1)))[:, None]
    cotangent = grad_out.astype(jnp.float32)[:, None]
    taps = lax.conv_general_dilated(padded, cotangent, (1, 1, 1), "VALID", dimension_numbers=("NCDHW", "OIDHW", "CDHWN"), precision=lax.Precision.HIGHEST)
    grad_w = taps.reshape(COUT, 27, CIN)
    return output, grad_w
```

```python
import jax
import jax.numpy as jnp
from jax import lax
from jax.experimental import pallas as pl
from jax.experimental.pallas import tpu as pltpu
from jax.sharding import PartitionSpec as P

F32 = jnp.float32
BF16 = jnp.bfloat16
Y_FIRST = ((0, 1, 2), ())
MESH = pl.DeviceIdType.MESH


def padded_2(block, sides, width):
    for axis, dim in sides:
        count = lax.axis_size(axis)
        forward = [(i, i + 1) for i in range(count - 1)]
        backward = [(target, source) for source, target in forward]
        low = lax.ppermute(
            lax.slice_in_dim(block, block.shape[dim] - width, None, axis=dim), axis, forward
        )
        high = lax.ppermute(lax.slice_in_dim(block, 0, width, axis=dim), axis, backward)
        block = jnp.concatenate([low, block, high], axis=dim)
    return block


def general_body(volume, weights, bias, grad_out):
    channels = volume.shape[0]
    rimmed = padded_2(volume, (("filt", 2), ("depth", 1)), 1)
    padded = jnp.pad(rimmed, ((0, 0), (0, 0), (0, 0), (1, 1)))
    stacked = padded[None]
    per_channel = padded[:, None]
    piece = lax.all_gather(weights, "filt", axis=0, tiled=True)
    count = piece.shape[0]
    kernel = piece.reshape(count, 3, 3, 3, channels)
    result = lax.conv_general_dilated(
        stacked,
        kernel,
        (1, 1, 1),
        "VALID",
        dimension_numbers=("NCDHW", "ODHWI", "NCDHW"),
        preferred_element_type=jnp.float32,
    )
    output = (result[0] + bias[:, None, None, None]).astype(jnp.bfloat16)
    all_filters = grad_out.shape[0]
    taps = lax.conv_general_dilated(
        per_channel,
        grad_out[:, None],
        (1, 1, 1),
        "VALID",
        dimension_numbers=("NCDHW", "OIDHW", "CDHWN"),
        preferred_element_type=jnp.float32,
    )
    term = taps.reshape(all_filters, 27, channels)
    summed = lax.psum(term, "depth")
    grad_w = lax.psum_scatter(summed, "filt", scatter_dimension=0, tiled=True)
    return (output, grad_w)


REACH = 6.0 * 65536
TOP = 2.0 ** 17.5


def fused_kernel(
    v_ref, w_ref, b_ref, g_ref,
    out_ref, gw_ref,
    vp, g3, wg, w9, part, ra, e1, r1, b1, e2, r2, b2, e3, r3, gs, most, seen,
    hs, hr, ws, wr, rs_s, rs_r, zs, zr, ms, mr,
):
    me = lax.axis_index("filt")
    core = lax.axis_index("depth")
    other = 1 - core
    xi = me % 2
    yi = (me // 2) % 2
    zi = me // 4
    x_peer = me + 1 - 2 * xi
    y_peer = me + 2 - 4 * yi
    xy_peer = zi * 4 + 3 - 2 * yi - xi
    z_to = [(zi + k) % 4 for k in (1, 2, 3)]
    z_peer = [t * 4 + yi * 2 + xi for t in z_to]
    far_peer = me - 1 + 2 * xi
    has_far = jnp.logical_and(me > 0, me < 15)
    near_slot, far_slot = 5 - 5 * xi, 5 * xi

    def dev(filt, depth=None):
        return {"filt": filt, "depth": core if depth is None else depth}

    def copy(src, dst, s_sem, r_sem, device):
        return pltpu.make_async_remote_copy(
            src_ref=src, dst_ref=dst, send_sem=s_sem, recv_sem=r_sem,
            device_id=device, device_id_type=MESH,
        )

    barrier = pltpu.get_barrier_semaphore()

    def greet(device):
        pl.semaphore_signal(barrier, inc=1, device_id=device, device_id_type=MESH)

    greet(dev(me, other))
    greet(dev(x_peer))
    greet(dev(y_peer))
    greet(dev(xy_peer))
    for p in z_peer:
        greet(dev(p))

    @pl.when(has_far)
    def _():
        greet(dev(far_peer))

    most[0] = jnp.max(
        jnp.abs(g_ref[...].astype(F32)).reshape(256, 8, 128), axis=0
    )
    pl.semaphore_wait(barrier, 6 + jnp.minimum(me, 1) + jnp.minimum(15 - me, 1))

    m_p = [
        copy(most.at[0], seen.at[k], ms.at[k], mr.at[k], dev(p))
        for k, p in enumerate((x_peer, y_peer, xy_peer))
    ]
    m_z = [
        copy(most.at[1], seen.at[3 + k], ms.at[3 + k], mr.at[3 + k], dev(p))
        for k, p in enumerate(z_peer)
    ]
    m_c = copy(most.at[2], seen.at[6], ms.at[6], mr.at[6], dev(me, other))
    for c in m_p:
        c.start()
    w_x = copy(w_ref.at[core], wg.at[core, yi, zi, xi], ws.at[3], wr.at[3], dev(x_peer))
    w_x.start()

    near = copy(v_ref.at[:, near_slot * 3 // 5], vp.at[1:5, 5 - near_slot], hs.at[0], hr.at[0], dev(x_peer))
    far = copy(v_ref.at[:, far_slot * 3 // 5], vp.at[1:5, 5 - far_slot], hs.at[1], hr.at[1], dev(far_peer))
    near.start()

    @pl.when(has_far)
    def _():
        far.start()

    my_edge = 3 - 3 * core
    send_slot = 5 - 5 * other
    inner = copy(v_ref.at[my_edge], vp.at[send_slot, 1:5], hs.at[2], hr.at[2], dev(me, other))
    inner.start()
    wg[core, yi, zi, xi] = w_ref[core]

    vp[1:5, 1:5] = v_ref[...]
    empty = 5 - 5 * (1 - core)
    vp[empty] = jnp.zeros((6, 256, 128), BF16)

    @pl.when(jnp.logical_not(has_far))
    def _():
        vp[1:5, far_slot] = jnp.zeros((4, 256, 128), BF16)
        vp[send_slot, far_slot] = jnp.zeros((256, 128), BF16)

    lane = lax.broadcasted_iota(jnp.int32, (128, 128), 1)
    for z in range(4):
        for x in range(4):
            cols = slice(x * 128, x * 128 + 128)
            g = g_ref[z, x]
            gf = g.astype(F32)
            up = jnp.where(lane == 127, 0.0, pltpu.roll(gf, 127, 1))
            down = jnp.where(lane == 0, 0.0, pltpu.roll(gf, 1, 1))
            g3[z, 0:128, cols] = up.astype(BF16)
            g3[z, 128:256, cols] = g
            g3[z, 256:384, cols] = down.astype(BF16)

    w_z = [
        copy(wg.at[core, yi, zi], wg.at[core, yi, zi], ws.at[k], wr.at[k], dev(z_peer[k]))
        for k in range(3)
    ]
    w_y = [
        copy(wg.at[core, yi, z], wg.at[core, yi, z], ws.at[6 + k], wr.at[6 + k], dev(y_peer))
        for k, z in enumerate([zi] + [(zi - k) % 4 for k in (1, 2, 3)])
    ]
    w_c = [
        copy(wg.at[core, row], wg.at[core, row], ws.at[4 + k], wr.at[4 + k], dev(me, other))
        for k, row in enumerate((yi, 1 - yi))
    ]

    def tap(j):
        dz, at = j
        return dz * 3 + (1, 2 - 2 * xi, 2 * xi)[at]

    def grad(j):
        dz = j[0]
        dx = tap(j) - 3 * dz
        total = None
        for z in range(4):
            term = lax.dot_general(
                g3[z], jnp.concatenate([vp[z + dz, dx + x] for x in range(4)], axis=1),
                (((1,), (1,)), ((), ())), preferred_element_type=F32,
            )
            total = term if total is None else total + term
        for h in range(2):
            blocks = total[:, h * 128 : h * 128 + 128].reshape(3, 4, 2, 2, 8, 128)
            for y in range(2):
                for x in range(2):
                    for dy in range(3):
                        first, second = (x, y) if not y_first(j) else (y, x)
                        part[tap(j), h, first, second, :, dy] = blocks[dy, :, y, x]

    def encode(value):
        t = value * most[0, 0:1, 0:1]
        a = t * t
        return (a * a * (a * t)).astype(BF16)

    def decode(coded):
        value = coded.astype(F32)
        size = jnp.exp2(jnp.log2(jnp.abs(value)) * (1.0 / 7.0)) * most[1, 0:1, 0:1]
        return jnp.where(value < 0, -size, size)

    def stage_a(j):
        i = tap(j)
        return copy(part.at[i, other], ra.at[i], rs_s.at[0, i], rs_r.at[0, i], dev(me, other))

    def y_first(j):
        return j[0] in Y_FIRST[j[1] > 0]

    def path(j):
        return ((xi, x_peer), (yi, y_peer)) if not y_first(j) else ((yi, y_peer), (xi, x_peer))

    def stage_1(j):
        i = tap(j)
        return copy(e1.at[i], r1.at[i], rs_s.at[1, i], rs_r.at[1, i], dev(path(j)[0][1]))

    def stage_2(j):
        i = tap(j)
        return copy(e2.at[i], r2.at[i], rs_s.at[2, i], rs_r.at[2, i], dev(path(j)[1][1]))

    def stage_3(j):
        i = tap(j)
        return [
            copy(e3.at[i, z_to[k]], r3.at[i, k], zs.at[i, k], zr.at[i, k], dev(z_peer[k]))
            for k in range(3)
        ]

    def after_a(j):
        i = tap(j)
        stage_a(j).wait_recv()
        side = path(j)[0][0]
        away = ra[i, 1 - side] + part[i, core, 1 - side]
        e1[i] = encode(away.reshape(192, 128))
        stage_1(j).start()
        b1[i] = ra[i, side] + part[i, core, side]

    def after_1(j):
        i = tap(j)
        stage_1(j).wait_recv()
        b1[i] = b1[i] + decode(r1[i]).reshape(2, 4, 3, 8, 128)
        side = path(j)[1][0]
        e2[i] = encode(b1[i, 1 - side].reshape(96, 128))
        stage_2(j).start()

    def after_2(j):
        i = tap(j)
        stage_2(j).wait_recv()
        side = path(j)[1][0]
        b1[i, side] = b1[i, side] + decode(r2[i]).reshape(4, 3, 8, 128)
        blank = jnp.zeros((8, 128), BF16)
        for k, c in enumerate(stage_3(j)):
            coded = encode(b1[i, side, z_to[k]].reshape(24, 128))
            e3[i, z_to[k]] = jnp.concatenate([coded, blank], axis=0)
            c.start()
        b2[i] = b1[i, side, zi].reshape(24, 128)

    def after_3(j):
        i = tap(j)
        total = b2[i]
        for k, c in enumerate(stage_3(j)):
            c.wait_recv()
            total = total + decode(r3[i, k])[0:24]
        gs[core, pl.ds(3 * i, 3)] = total.reshape(3, 8, 128)

    def arrange():
        for h in range(2):
            for z in range(4):
                for y in range(2):
                    pair = [wg[h, y, z, x].astype(F32).reshape(27, 8, 128) for x in range(2)]
                    rows = jnp.concatenate(pair, axis=1).astype(BF16).reshape(9, 3, 16, 128)
                    at = 16 * (2 * z + y)
                    for dy in range(3):
                        w9[:, dy * 128 + at : dy * 128 + at + 16, h * 128 : h * 128 + 128] = rows[:, dy]

    def forward(u):
        z, half = u // 2, u % 2
        total = None
        for dz in range(3):
            for dx in range(3):
                at = dx + 2 * half
                cells = jnp.concatenate([vp[z + dz, at], vp[z + dz, at + 1]], axis=1)
                term = jnp.dot(w9[dz * 3 + dx], cells, preferred_element_type=F32)
                total = term if total is None else total + term
        for x in range(2):
            cols = slice(x * 128, x * 128 + 128)
            low = jnp.where(lane == 0, 0.0, pltpu.roll(total[0:128, cols], 1, 1))
            high = jnp.where(lane == 127, 0.0, pltpu.roll(total[256:384, cols], 127, 1))
            value = low + total[128:256, cols] + high + b_ref[...]
            out_ref[z, x + 2 * half] = value.astype(BF16)

    edge_slot = 4 - 3 * core
    near_corner = copy(vp.at[edge_slot, near_slot], vp.at[send_slot, near_slot], hs.at[3], hr.at[3], dev(me, other))
    far_corner = copy(vp.at[edge_slot, far_slot], vp.at[send_slot, far_slot], hs.at[4], hr.at[4], dev(me, other))

    def near_rim():
        near.wait_recv()
        near_corner.start()

    def far_rim():
        @pl.when(has_far)
        def _():
            far.wait_recv()
            far_corner.start()

    def far_edge():
        @pl.when(has_far)
        def _():
            far_corner.wait_recv()

    def chunk(j):
        grad(j)
        stage_a(j).start()

    def scale_line():
        for c in m_p:
            c.wait_recv()
        most[1] = jnp.maximum(jnp.maximum(most[0], seen[0]), jnp.maximum(seen[1], seen[2]))
        for c in m_z:
            c.start()

    def scale_chip():
        for c in m_z:
            c.wait_recv()
        most[2] = jnp.maximum(jnp.maximum(most[1], seen[3]), jnp.maximum(seen[4], seen[5]))
        m_c.start()

    def scale_all():
        m_c.wait_recv()
        top = jnp.maximum(most[2], seen[6])
        top = jnp.max(top, axis=0, keepdims=True)
        top = jnp.maximum(jnp.max(top, axis=1, keepdims=True), 1e-30)
        for c in m_p + m_z + [m_c]:
            c.wait_send()
        most[0] = jnp.broadcast_to((TOP / REACH) / top, (8, 128))
        most[1] = jnp.broadcast_to(top * (REACH / TOP), (8, 128))

    def spread(k):
        w_z[k].wait_recv()
        w_y[k + 1].start()

    mid, near_1, far_1 = [[(dz, at) for dz in (1, 0, 2)] for at in (0, 1, 2)]
    scale_line()
    w_x.wait_recv()
    for c in w_z:
        c.start()
    w_y[0].start()
    inner.wait_recv()
    chunk(mid[0])
    chunk(mid[1])
    scale_chip()
    chunk(mid[2])
    scale_all()
    for j in mid:
        after_a(j)
    spread(0)
    near_rim()
    chunk(near_1[0])
    after_1(mid[0])
    near_corner.wait_recv()
    chunk(near_1[1])
    after_a(near_1[0])
    after_1(mid[1])
    chunk(near_1[2])
    after_a(near_1[1])
    after_1(mid[2])
    after_a(near_1[2])
    spread(1)
    spread(2)
    w_c[0].start()
    far_rim()
    chunk(far_1[0])
    far_edge()
    chunk(far_1[1])
    after_a(far_1[0])
    chunk(far_1[2])
    after_a(far_1[1])
    after_1(far_1[0])
    after_a(far_1[2])
    after_1(far_1[1])
    after_2(mid[0])
    after_1(far_1[2])
    after_2(mid[1])
    after_2(mid[2])
    after_1(near_1[0])
    after_2(far_1[0])
    after_1(near_1[1])
    after_2(far_1[1])
    after_1(near_1[2])
    after_2(far_1[2])
    for c in w_y:
        c.wait_recv()
    w_c[1].start()
    after_2(near_1[0])
    after_3(mid[0])
    after_2(near_1[1])
    after_3(mid[1])
    after_3(mid[2])
    after_2(near_1[2])
    for c in w_c:
        c.wait_recv()
    arrange()
    for u in range(3):
        forward(u)
    after_3(far_1[0])
    forward(3)
    after_3(far_1[1])
    forward(4)
    after_3(far_1[2])
    forward(5)
    after_3(near_1[0])
    forward(6)
    after_3(near_1[1])
    after_3(near_1[2])
    last = copy(gs.at[core], gs.at[core], hs.at[5], hr.at[5], dev(me, other))
    last.start()
    forward(7)
    near.wait_send()
    near_corner.wait_send()

    @pl.when(has_far)
    def _():
        far.wait_send()
        far_corner.wait_send()

    inner.wait_send()
    for c in w_z + w_y + w_c + [w_x]:
        c.wait_send()
    for j in mid + near_1 + far_1:
        stage_a(j).wait_send()
        stage_1(j).wait_send()
        stage_2(j).wait_send()
        for c in stage_3(j):
            c.wait_send()
    last.wait()
    for h in range(2):
        gw_ref[:, :, h * 128 : h * 128 + 128] = gs[h]


def fused_body(volume, weights, bias, grad_out):
    v = volume.transpose(1, 2, 0, 3)
    g = grad_out.transpose(1, 2, 0, 3)
    w = weights.reshape(8, 27, 2, 128).transpose(2, 1, 0, 3).reshape(2, 216, 128)
    b = jnp.broadcast_to(bias[:, None], (128, 128))
    vmem = pl.BlockSpec(memory_space=pltpu.VMEM)
    dma = pltpu.SemaphoreType.DMA
    out, gw = pl.pallas_call(
        fused_kernel,
        out_shape=(
            jax.ShapeDtypeStruct((4, 4, 128, 128), BF16),
            jax.ShapeDtypeStruct((27, 8, 256), F32),
        ),
        in_specs=[vmem] * 4,
        out_specs=(vmem, vmem),
        scratch_shapes=[
            pltpu.VMEM((6, 6, 256, 128), BF16),
            pltpu.VMEM((4, 384, 512), BF16),
            pltpu.VMEM((2, 2, 4, 2, 216, 128), BF16),
            pltpu.VMEM((9, 384, 256), BF16),
            pltpu.VMEM((9, 2, 2, 2, 4, 3, 8, 128), F32),
            pltpu.VMEM((9, 2, 2, 4, 3, 8, 128), F32),
            pltpu.VMEM((9, 192, 128), BF16),
            pltpu.VMEM((9, 192, 128), BF16),
            pltpu.VMEM((9, 2, 4, 3, 8, 128), F32),
            pltpu.VMEM((9, 96, 128), BF16),
            pltpu.VMEM((9, 96, 128), BF16),
            pltpu.VMEM((9, 24, 128), F32),
            pltpu.VMEM((9, 4, 32, 128), BF16),
            pltpu.VMEM((9, 3, 32, 128), BF16),
            pltpu.VMEM((2, 27, 8, 128), F32),
            pltpu.VMEM((3, 8, 128), F32),
            pltpu.VMEM((7, 8, 128), F32),
            dma((6,)), dma((6,)), dma((10,)), dma((10,)),
            dma((3, 9)), dma((3, 9)), dma((9, 3)), dma((9, 3)),
            dma((7,)), dma((7,)),
        ],
        compiler_params=pltpu.CompilerParams(
            collective_id=0, has_side_effects=True, vmem_limit_bytes=48 << 20
        ),
    )(v, w, b, g)
    output = out.transpose(2, 0, 1, 3)
    grad_w = gw.transpose(1, 0, 2)
    return (output, grad_w)


def solution(mesh):
    in_specs = (
        P(None, "depth", "filt", None),
        P("filt", None, None),
        P(),
        P(None, "depth", "filt", None),
    )
    out_specs = (P(None, "depth", "filt", None), P("filt", None, None))
    small = mesh.shape["filt"] == 16 and mesh.shape["depth"] == 2

    def body(volume, weights, bias, grad_out):
        shapes = (volume.shape, weights.shape, grad_out.shape)
        if small and shapes == ((256, 4, 4, 128), (8, 27, 256), (128, 4, 4, 128)):
            return fused_body(volume, weights, bias, grad_out)
        return general_body(volume, weights, bias, grad_out)

    return jax.shard_map(body, mesh=mesh, in_specs=in_specs, out_specs=out_specs, check_vma=False)
```

```python
import jax
import jax.numpy as jnp
from jax import lax
from jax.experimental import pallas as pl
from jax.experimental.pallas import tpu as pltpu
from jax.sharding import PartitionSpec as P

F32 = jnp.float32
BF16 = jnp.bfloat16
Y_FIRST = ((0, 1, 2), ())
MESH = pl.DeviceIdType.MESH


def padded_2(block, sides, width):
    for axis, dim in sides:
        count = lax.axis_size(axis)
        forward = [(i, i + 1) for i in range(count - 1)]
        backward = [(target, source) for source, target in forward]
        low = lax.ppermute(
            lax.slice_in_dim(block, block.shape[dim] - width, None, axis=dim), axis, forward
        )
        high = lax.ppermute(lax.slice_in_dim(block, 0, width, axis=dim), axis, backward)
        block = jnp.concatenate([low, block, high], axis=dim)
    return block


def general_body(volume, weights, bias, grad_out):
    channels = volume.shape[0]
    rimmed = padded_2(volume, (("filt", 2), ("depth", 1)), 1)
    padded = jnp.pad(rimmed, ((0, 0), (0, 0), (0, 0), (1, 1)))
    stacked = padded[None]
    per_channel = padded[:, None]
    piece = lax.all_gather(weights, "filt", axis=0, tiled=True)
    count = piece.shape[0]
    kernel = piece.reshape(count, 3, 3, 3, channels)
    result = lax.conv_general_dilated(
        stacked,
        kernel,
        (1, 1, 1),
        "VALID",
        dimension_numbers=("NCDHW", "ODHWI", "NCDHW"),
        preferred_element_type=jnp.float32,
    )
    output = (result[0] + bias[:, None, None, None]).astype(jnp.bfloat16)
    all_filters = grad_out.shape[0]
    taps = lax.conv_general_dilated(
        per_channel,
        grad_out[:, None],
        (1, 1, 1),
        "VALID",
        dimension_numbers=("NCDHW", "OIDHW", "CDHWN"),
        preferred_element_type=jnp.float32,
    )
    term = taps.reshape(all_filters, 27, channels)
    summed = lax.psum(term, "depth")
    grad_w = lax.psum_scatter(summed, "filt", scatter_dimension=0, tiled=True)
    return (output, grad_w)


REACH = 6.0 * 65536
TOP = 2.0 ** 17.5


def fused_kernel(
    v_hbm, w_hbm, b_hbm, g_hbm,
    out_ref, gw_ref,
    vp, g3, wg, w9, part, ra, e1, r1, b1, e2, r2, b2, e3, r3, gs, most, scale,
    hs, hr, ws, wr, rs_s, rs_r, zs, zr, ms, mr, bias, wide, v_in, g_in, b_in, v_wide, loads,
):
    me = lax.axis_index("filt")
    core = lax.axis_index("depth")
    other = 1 - core
    xi = me % 2
    yi = (me // 2) % 2
    zi = me // 4
    x_peer = me + 1 - 2 * xi
    y_peer = me + 2 - 4 * yi
    z_to = [(zi + k) % 4 for k in (1, 2, 3)]
    z_peer = [t * 4 + yi * 2 + xi for t in z_to]
    far_peer = me - 1 + 2 * xi
    has_far = jnp.logical_and(me > 0, me < 15)
    near_slot, far_slot = 5 - 5 * xi, 5 * xi

    def dev(filt, depth=None):
        return {"filt": filt, "depth": core if depth is None else depth}

    def copy(src, dst, s_sem, r_sem, device):
        return pltpu.make_async_remote_copy(
            src_ref=src, dst_ref=dst, send_sem=s_sem, recv_sem=r_sem,
            device_id=device, device_id_type=MESH,
        )

    v_load = pltpu.make_async_copy(v_hbm, v_in, loads.at[0])
    g_load = pltpu.make_async_copy(g_hbm, g_in, loads.at[1])
    b_load = pltpu.make_async_copy(b_hbm, b_in, loads.at[2])
    half = pl.ds(pl.multiple_of(core * 128, 128), 128)
    w_load = pltpu.make_async_copy(w_hbm.at[:, half], wg.at[core, yi, zi, xi], loads.at[3])
    v_load.start()
    w_load.start()
    g_load.start()
    b_load.start()
    barrier = pltpu.get_barrier_semaphore()

    def greet(device):
        pl.semaphore_signal(barrier, inc=1, device_id=device, device_id_type=MESH)

    greet(dev(me, other))
    greet(dev(x_peer))
    greet(dev(y_peer))
    for p in z_peer:
        greet(dev(p))

    @pl.when(has_far)
    def _():
        greet(dev(far_peer))

    def place(z, x):
        vp[z + 1, x + 1] = v_wide[pl.ds(4 * z + x, 256, stride=16), :].astype(BF16)

    v_load.wait()
    v_wide[...] = v_in[...].astype(F32)
    for z in range(4):
        place(z, 0)
        place(z, 3)
    pl.semaphore_wait(barrier, 5 + jnp.minimum(me, 1) + jnp.minimum(15 - me, 1))

    w_x = copy(wg.at[core, yi, zi, xi], wg.at[core, yi, zi, xi], ws.at[3], wr.at[3], dev(x_peer))
    w_load.wait()
    w_x.start()

    near = copy(vp.at[1:5, 4 - 3 * xi], vp.at[1:5, 5 * xi], hs.at[0], hr.at[0], dev(x_peer))
    far = copy(vp.at[1:5, 1 + 3 * xi], vp.at[1:5, 5 - 5 * xi], hs.at[1], hr.at[1], dev(far_peer))

    @pl.when(has_far)
    def _():
        far.start()

    near.start()
    for z in range(4):
        place(z, 1)
        place(z, 2)
    my_edge = 3 - 3 * core
    send_slot = 5 - 5 * other
    inner = copy(vp.at[my_edge + 1, 1:5], vp.at[send_slot, 1:5], hs.at[2], hr.at[2], dev(me, other))
    inner.start()
    g_load.wait()
    wide[...] = g_in[...].astype(F32)
    top = jnp.max(jnp.abs(wide[...]).reshape(256, 8, 128), axis=0)
    top = jnp.max(jnp.max(top, axis=0, keepdims=True), axis=1, keepdims=True)
    most[0] = jnp.broadcast_to(jnp.maximum(top, 2.0 ** -100), (8, 128))
    share = copy(most.at[0], most.at[1], ms, mr, dev(me, other))
    share.start()
    b_load.wait()
    bias[...] = jnp.broadcast_to(b_in[...], (128, 128)).T.reshape(4, 2, 16, 128)
    empty = 5 - 5 * (1 - core)
    vp[empty] = jnp.zeros((6, 256, 128), BF16)

    @pl.when(jnp.logical_not(has_far))
    def _():
        vp[1:5, far_slot] = jnp.zeros((4, 256, 128), BF16)
        vp[send_slot, far_slot] = jnp.zeros((256, 128), BF16)

    lane = lax.broadcasted_iota(jnp.int32, (128, 128), 1)
    for z in range(4):
        for x in range(4):
            cols = slice(x * 128, x * 128 + 128)
            gf = wide[pl.ds(4 * z + x, 128, stride=16), :]
            up = jnp.where(lane == 127, 0.0, pltpu.roll(gf, 127, 1))
            down = jnp.where(lane == 0, 0.0, pltpu.roll(gf, 1, 1))
            g3[z, 0:128, cols] = up.astype(BF16)
            g3[z, 128:256, cols] = gf.astype(BF16)
            g3[z, 256:384, cols] = down.astype(BF16)

    w_z = [
        copy(wg.at[core, yi, zi], wg.at[core, yi, zi], ws.at[k], wr.at[k], dev(z_peer[k]))
        for k in range(3)
    ]
    w_y = [
        copy(wg.at[core, yi, z], wg.at[core, yi, z], ws.at[6 + k], wr.at[6 + k], dev(y_peer))
        for k, z in enumerate([zi] + [(zi - k) % 4 for k in (1, 2, 3)])
    ]
    w_c = [
        copy(wg.at[core, row], wg.at[core, row], ws.at[4 + k], wr.at[4 + k], dev(me, other))
        for k, row in enumerate((yi, 1 - yi))
    ]

    def tap(j):
        dz, at = j
        return dz * 3 + (1, 2 - 2 * xi, 2 * xi)[at]

    def grad(j):
        dz = j[0]
        dx = tap(j) - 3 * dz
        total = None
        for z in range(4):
            term = lax.dot_general(
                g3[z], jnp.concatenate([vp[z + dz, dx + x] for x in range(4)], axis=1),
                (((1,), (1,)), ((), ())), preferred_element_type=F32,
            )
            total = term if total is None else total + term
        for h in range(2):
            blocks = total[:, h * 128 : h * 128 + 128].reshape(3, 4, 2, 2, 8, 128)
            for y in range(2):
                for x in range(2):
                    for dy in range(3):
                        first, second = (x, y) if not y_first(j) else (y, x)
                        part[tap(j), h, first, second, :, dy] = blocks[dy, :, y, x]

    def encode(value, bound):
        t = value.reshape(-1, 8, 128) * ((TOP / REACH) / bound)
        a = t * t
        coded = (a * a * (a * t)).reshape(value.shape)
        ends = [bound] if value.shape[0] % 16 else [bound, bound]
        return jnp.concatenate([coded] + ends, axis=0).astype(BF16)

    def decode(coded, count):
        value = coded.astype(F32).reshape(-1, 8, 128)
        bound = value[count]
        value = value[:count]
        size = jnp.exp2(jnp.log2(jnp.abs(value)) * (1.0 / 7.0)) * (bound * (REACH / TOP))
        return jnp.where(value < 0, -size, size), bound

    def stage_a(j):
        i = tap(j)
        return copy(part.at[i, other], ra.at[i], rs_s.at[0, i], rs_r.at[0, i], dev(me, other))

    def y_first(j):
        return j[0] in Y_FIRST[j[1] > 0]

    def path(j):
        return ((xi, x_peer), (yi, y_peer)) if not y_first(j) else ((yi, y_peer), (xi, x_peer))

    def stage_1(j):
        i = tap(j)
        return copy(e1.at[i], r1.at[i], rs_s.at[1, i], rs_r.at[1, i], dev(path(j)[0][1]))

    def stage_2(j):
        i = tap(j)
        return copy(e2.at[i], r2.at[i], rs_s.at[2, i], rs_r.at[2, i], dev(path(j)[1][1]))

    def stage_3(j):
        i = tap(j)
        return [
            copy(e3.at[i, z_to[k]], r3.at[i, k], zs.at[i, k], zr.at[i, k], dev(z_peer[k]))
            for k in range(3)
        ]

    def after_a(j):
        i = tap(j)
        stage_a(j).wait_recv()
        side = path(j)[0][0]
        away = ra[i, 1 - side] + part[i, core, 1 - side]
        e1[i] = encode(away.reshape(192, 128), most[2])
        stage_1(j).start()
        b1[i] = ra[i, side] + part[i, core, side]

    def after_1(j):
        i = tap(j)
        stage_1(j).wait_recv()
        value, bound = decode(r1[i], 24)
        bound = jnp.maximum(bound, most[2])
        scale[i] = bound
        side = path(j)[1][0]
        value = value.reshape(2, 4, 3, 8, 128)
        b1[i] = b1[i] + value
        e2[i] = encode(b1[i, 1 - side].reshape(96, 128), bound)
        stage_2(j).start()

    def after_2(j):
        i = tap(j)
        stage_2(j).wait_recv()
        side = path(j)[1][0]
        value, bound = decode(r2[i], 12)
        bound = jnp.maximum(bound, scale[i])
        b1[i, side] = b1[i, side] + value.reshape(4, 3, 8, 128)
        for k, c in enumerate(stage_3(j)):
            e3[i, z_to[k]] = encode(b1[i, side, z_to[k]].reshape(24, 128), bound)
            c.start()
        b2[i] = b1[i, side, zi]

    def after_3(j):
        i = tap(j)
        total = b2[i]
        for k, c in enumerate(stage_3(j)):
            c.wait_recv()
            total = total + decode(r3[i, k], 3)[0]
        gs[core, pl.ds(3 * i, 3)] = total

    def arrange(row):
        for h in range(2):
            for z in range(4):
                pair = [wg[h, row, z, x].astype(F32).reshape(27, 8, 128) for x in range(2)]
                rows = jnp.concatenate(pair, axis=1).astype(BF16).reshape(9, 3, 16, 128)
                for dy in range(3):
                    at = dy * 64 + z * 16
                    w9[row, :, at : at + 16, h * 128 : h * 128 + 128] = rows[:, dy]

    def forward(row, u):
        z, half = u // 2, u % 2
        total = None
        for dz in range(3):
            for dx in range(3):
                at = dx + 2 * half
                cells = jnp.concatenate([vp[z + dz, at], vp[z + dz, at + 1]], axis=1)
                term = jnp.dot(w9[row, dz * 3 + dx], cells, preferred_element_type=F32)
                total = term if total is None else total + term
        edge = lane[0:64]
        for x in range(2):
            cols = slice(x * 128, x * 128 + 128)
            low = jnp.where(edge == 0, 0.0, pltpu.roll(total[0:64, cols], 1, 1))
            high = jnp.where(edge == 127, 0.0, pltpu.roll(total[128:192, cols], 127, 1))
            value = low + total[64:128, cols] + high + bias[:, row].reshape(64, 128)
            for part_z in range(4):
                at = (part_z * 32 + row * 16) * 16 + 4 * z + x + 2 * half
                wide[pl.ds(at, 16, stride=16), :] = value[part_z * 16 : part_z * 16 + 16]

    edge_slot = 4 - 3 * core
    near_corner = copy(vp.at[edge_slot, near_slot], vp.at[send_slot, near_slot], hs.at[3], hr.at[3], dev(me, other))
    far_corner = copy(vp.at[edge_slot, far_slot], vp.at[send_slot, far_slot], hs.at[4], hr.at[4], dev(me, other))

    def near_rim():
        near.wait_recv()
        near_corner.start()

    def far_rim():
        @pl.when(has_far)
        def _():
            far.wait_recv()
            far_corner.start()

    def far_edge():
        @pl.when(has_far)
        def _():
            far_corner.wait_recv()

    def chunk(j):
        grad(j)
        stage_a(j).start()

    def spread(k):
        w_z[k].wait_recv()
        w_y[k + 1].start()

    mid, near_1, far_1 = [[(dz, at) for dz in (1, 0, 2)] for at in (0, 1, 2)]
    inner.wait_recv()
    chunk(mid[0])
    share.wait_recv()
    most[2] = jnp.maximum(most[0], most[1])
    chunk(mid[1])
    w_x.wait_recv()
    for c in w_z:
        c.start()
    w_y[0].start()
    after_a(mid[0])
    chunk(mid[2])
    after_a(mid[1])
    after_a(mid[2])
    far_rim()
    chunk(far_1[0])
    far_edge()
    chunk(far_1[1])
    after_a(far_1[0])
    after_1(mid[0])
    chunk(far_1[2])
    after_a(far_1[1])
    after_1(mid[1])
    after_a(far_1[2])
    after_1(mid[2])
    spread(0)
    near_rim()
    chunk(near_1[0])
    near_corner.wait_recv()
    chunk(near_1[1])
    after_a(near_1[0])
    chunk(near_1[2])
    after_a(near_1[1])
    after_a(near_1[2])
    spread(1)
    spread(2)
    w_c[0].start()
    after_1(near_1[0])
    after_2(mid[0])
    after_1(near_1[1])
    after_2(mid[1])
    after_1(near_1[2])
    after_2(mid[2])
    w_c[0].wait_recv()
    arrange(yi)
    after_1(far_1[0])
    forward(yi, 0)
    after_1(far_1[1])
    forward(yi, 1)
    after_1(far_1[2])
    after_2(near_1[0])
    forward(yi, 2)
    after_2(near_1[1])
    forward(yi, 3)
    after_2(near_1[2])
    for c in w_y:
        c.wait_recv()
    w_c[1].start()
    forward(yi, 4)
    after_2(far_1[0])
    forward(yi, 5)
    after_2(far_1[1])
    forward(yi, 6)
    after_2(far_1[2])
    forward(yi, 7)
    w_c[1].wait_recv()
    arrange(1 - yi)
    for j in mid:
        after_3(j)
    for u in range(4):
        forward(1 - yi, u)
    for j in near_1:
        after_3(j)
    forward(1 - yi, 4)
    after_3(far_1[0])
    forward(1 - yi, 5)
    after_3(far_1[1])
    after_3(far_1[2])
    last = copy(gs.at[core], gs.at[core], hs.at[5], hr.at[5], dev(me, other))
    last.start()
    forward(1 - yi, 6)
    forward(1 - yi, 7)
    out_ref[...] = wide[...].astype(BF16)
    near.wait_send()
    near_corner.wait_send()
    share.wait_send()

    @pl.when(has_far)
    def _():
        far.wait_send()
        far_corner.wait_send()

    inner.wait_send()
    for c in w_z + w_y + w_c + [w_x]:
        c.wait_send()
    for j in mid + near_1 + far_1:
        stage_a(j).wait_send()
        stage_1(j).wait_send()
        stage_2(j).wait_send()
        for c in stage_3(j):
            c.wait_send()
    last.wait()
    for h in range(2):
        gw_ref[:, :, h * 128 : h * 128 + 128] = gs[h]


def fused_body(volume, weights, bias, grad_out):
    v = volume.reshape(4096, 128)
    g = grad_out.reshape(2048, 128)
    w = weights.transpose(1, 0, 2).reshape(216, 256)
    b = bias.reshape(1, 128)
    vmem = pl.BlockSpec(memory_space=pltpu.VMEM)
    hold = lambda a: pltpu.with_memory_space_constraint(a, pltpu.HBM)
    hbm = pl.BlockSpec(memory_space=pltpu.HBM)
    dma = pltpu.SemaphoreType.DMA
    out, gw = pl.pallas_call(
        fused_kernel,
        out_shape=(
            jax.ShapeDtypeStruct((2048, 128), BF16),
            jax.ShapeDtypeStruct((27, 8, 256), F32),
        ),
        in_specs=[hbm] * 4,
        out_specs=(vmem, vmem),
        scratch_shapes=[
            pltpu.VMEM((6, 6, 256, 128), BF16),
            pltpu.VMEM((4, 384, 512), BF16),
            pltpu.VMEM((2, 2, 4, 2, 216, 128), BF16),
            pltpu.VMEM((2, 9, 192, 256), BF16),
            pltpu.VMEM((9, 2, 2, 2, 4, 3, 8, 128), F32),
            pltpu.VMEM((9, 2, 2, 4, 3, 8, 128), F32),
            pltpu.VMEM((9, 208, 128), BF16),
            pltpu.VMEM((9, 208, 128), BF16),
            pltpu.VMEM((9, 2, 4, 3, 8, 128), F32),
            pltpu.VMEM((9, 112, 128), BF16),
            pltpu.VMEM((9, 112, 128), BF16),
            pltpu.VMEM((9, 3, 8, 128), F32),
            pltpu.VMEM((9, 4, 32, 128), BF16),
            pltpu.VMEM((9, 3, 32, 128), BF16),
            pltpu.VMEM((2, 27, 8, 128), F32),
            pltpu.VMEM((3, 8, 128), F32),
            pltpu.VMEM((9, 8, 128), F32),
            dma((6,)), dma((6,)), dma((10,)), dma((10,)),
            dma((3, 9)), dma((3, 9)), dma((9, 3)), dma((9, 3)),
            dma, dma,
            pltpu.VMEM((4, 2, 16, 128), F32),
            pltpu.VMEM((2048, 128), F32),
            pltpu.VMEM((4096, 128), BF16),
            pltpu.VMEM((2048, 128), BF16),
            pltpu.VMEM((1, 128), F32),
            pltpu.VMEM((4096, 128), F32),
            dma((4,)),
        ],
        compiler_params=pltpu.CompilerParams(
            collective_id=0, has_side_effects=True, vmem_limit_bytes=48 << 20
        ),
    )(hold(v), hold(w), hold(b), hold(g))
    output = out.reshape(128, 4, 4, 128)
    grad_w = gw.transpose(1, 0, 2)
    return (output, grad_w)


def solution(mesh):
    in_specs = (
        P(None, "depth", "filt", None),
        P("filt", None, None),
        P(),
        P(None, "depth", "filt", None),
    )
    out_specs = (P(None, "depth", "filt", None), P("filt", None, None))
    small = mesh.shape["filt"] == 16 and mesh.shape["depth"] == 2

    def body(volume, weights, bias, grad_out):
        shapes = (volume.shape, weights.shape, grad_out.shape)
        if small and shapes == ((256, 4, 4, 128), (8, 27, 256), (128, 4, 4, 128)):
            return fused_body(volume, weights, bias, grad_out)
        return general_body(volume, weights, bias, grad_out)

    return jax.shard_map(body, mesh=mesh, in_specs=in_specs, out_specs=out_specs, check_vma=False)
```

```python
import jax
import jax.numpy as jnp
from jax import lax
from jax.experimental import pallas as pl
from jax.experimental.pallas import tpu as pltpu
from jax.sharding import PartitionSpec as P

F32 = jnp.float32
BF16 = jnp.bfloat16
Y_FIRST = ((0, 1, 2), ())
MESH = pl.DeviceIdType.MESH


def padded_2(block, sides, width):
    for axis, dim in sides:
        count = lax.axis_size(axis)
        forward = [(i, i + 1) for i in range(count - 1)]
        backward = [(target, source) for source, target in forward]
        low = lax.ppermute(
            lax.slice_in_dim(block, block.shape[dim] - width, None, axis=dim), axis, forward
        )
        high = lax.ppermute(lax.slice_in_dim(block, 0, width, axis=dim), axis, backward)
        block = jnp.concatenate([low, block, high], axis=dim)
    return block


def general_body(volume, weights, bias, grad_out):
    channels = volume.shape[0]
    rimmed = padded_2(volume, (("filt", 2), ("depth", 1)), 1)
    padded = jnp.pad(rimmed, ((0, 0), (0, 0), (0, 0), (1, 1)))
    stacked = padded[None]
    per_channel = padded[:, None]
    piece = lax.all_gather(weights, "filt", axis=0, tiled=True)
    count = piece.shape[0]
    kernel = piece.reshape(count, 3, 3, 3, channels)
    result = lax.conv_general_dilated(
        stacked,
        kernel,
        (1, 1, 1),
        "VALID",
        dimension_numbers=("NCDHW", "ODHWI", "NCDHW"),
        preferred_element_type=jnp.float32,
    )
    output = (result[0] + bias[:, None, None, None]).astype(jnp.bfloat16)
    all_filters = grad_out.shape[0]
    taps = lax.conv_general_dilated(
        per_channel,
        grad_out[:, None],
        (1, 1, 1),
        "VALID",
        dimension_numbers=("NCDHW", "OIDHW", "CDHWN"),
        preferred_element_type=jnp.float32,
    )
    term = taps.reshape(all_filters, 27, channels)
    summed = lax.psum(term, "depth")
    grad_w = lax.psum_scatter(summed, "filt", scatter_dimension=0, tiled=True)
    return (output, grad_w)


REACH = 6.0 * 65536
TOP = 2.0 ** 17.5


def fused_kernel(
    v_hbm, w_hbm, b_hbm, g_hbm,
    out_ref, gw_ref,
    vp, g3, wg, w9, part, ra, e1, r1, b1, e2, r2, e3, r3, gs, most, scale,
    hs, hr, ws, wr, rs_s, rs_r, zs, zr, ms, mr, bias, wide, v_in, g_in, b_in, v_wide, loads, held, ls, lr,
):
    me = lax.axis_index("filt")
    core = lax.axis_index("depth")
    other = 1 - core
    xi = me % 2
    yi = (me // 2) % 2
    zi = me // 4
    x_peer = me + 1 - 2 * xi
    y_peer = me + 2 - 4 * yi
    z_to = [(zi + k) % 4 for k in (1, 2, 3)]
    z_peer = [t * 4 + yi * 2 + xi for t in z_to]
    far_peer = me - 1 + 2 * xi
    has_far = jnp.logical_and(me > 0, me < 15)
    near_slot, far_slot = 5 - 5 * xi, 5 * xi

    def dev(filt, depth=None):
        return {"filt": filt, "depth": core if depth is None else depth}

    def copy(src, dst, s_sem, r_sem, device):
        return pltpu.make_async_remote_copy(
            src_ref=src, dst_ref=dst, send_sem=s_sem, recv_sem=r_sem,
            device_id=device, device_id_type=MESH,
        )

    v_load = pltpu.make_async_copy(v_hbm, v_in, loads.at[0])
    g_load = pltpu.make_async_copy(g_hbm, g_in, loads.at[1])
    b_load = pltpu.make_async_copy(b_hbm, b_in, loads.at[2])
    half = pl.ds(pl.multiple_of(core * 128, 128), 128)
    w_load = pltpu.make_async_copy(w_hbm.at[:, half], wg.at[core, yi, zi, xi], loads.at[3])
    v_load.start()
    w_load.start()
    g_load.start()
    b_load.start()
    barrier = pltpu.get_barrier_semaphore()

    def greet(device):
        pl.semaphore_signal(barrier, inc=1, device_id=device, device_id_type=MESH)

    greet(dev(me, other))
    greet(dev(x_peer))
    greet(dev(y_peer))
    for p in z_peer:
        greet(dev(p))

    @pl.when(has_far)
    def _():
        greet(dev(far_peer))

    def place(z, x):
        vp[z + 1, x + 1] = v_wide[pl.ds(4 * z + x, 256, stride=16), :].astype(BF16)

    v_load.wait()
    v_wide[...] = v_in[...].astype(F32)
    for z in range(4):
        place(z, 0)
        place(z, 3)
    pl.semaphore_wait(barrier, 5 + jnp.minimum(me, 1) + jnp.minimum(15 - me, 1))

    w_x = copy(wg.at[core, yi, zi, xi], wg.at[core, yi, zi, xi], ws.at[2, 0], wr.at[2, 0], dev(x_peer))
    w_load.wait()
    w_x.start()

    my_edge = 3 - 3 * core
    planes = (pl.ds(my_edge + 1, 1), pl.ds(1 + core, 3))
    near = [
        copy(vp.at[p, 4 - 3 * xi], vp.at[p, 5 * xi], hs.at[k], hr.at[k], dev(x_peer))
        for k, p in enumerate(planes)
    ]
    far = [
        copy(vp.at[p, 1 + 3 * xi], vp.at[p, 5 - 5 * xi], hs.at[6 + k], hr.at[6 + k], dev(far_peer))
        for k, p in enumerate(planes)
    ]

    @pl.when(has_far)
    def _():
        for c in far:
            c.start()

    for c in near:
        c.start()
    for z in range(4):
        place(z, 1)
        place(z, 2)
    send_slot = 5 - 5 * other
    inner = copy(vp.at[my_edge + 1, 1:5], vp.at[send_slot, 1:5], hs.at[2], hr.at[2], dev(me, other))
    inner.start()
    g_load.wait()
    wide[...] = g_in[...].astype(F32)
    top = jnp.max(jnp.abs(wide[...]).reshape(256, 8, 128), axis=0)
    top = jnp.max(jnp.max(top, axis=0, keepdims=True), axis=1, keepdims=True)
    most[0] = jnp.broadcast_to(jnp.maximum(top, 2.0 ** -100), (8, 128))
    share = copy(most.at[0], most.at[1], ms, mr, dev(me, other))
    share.start()
    b_load.wait()
    bias[...] = jnp.broadcast_to(b_in[...], (128, 128)).T.reshape(4, 2, 16, 128)
    empty = 5 - 5 * (1 - core)
    vp[empty] = jnp.zeros((6, 256, 128), BF16)

    @pl.when(jnp.logical_not(has_far))
    def _():
        vp[1:5, far_slot] = jnp.zeros((4, 256, 128), BF16)
        vp[send_slot, far_slot] = jnp.zeros((256, 128), BF16)

    lane = lax.broadcasted_iota(jnp.int32, (128, 128), 1)
    for z in range(4):
        for x in range(4):
            gf = wide[pl.ds(4 * z + x, 128, stride=16), :]
            up = jnp.where(lane == 127, 0.0, pltpu.roll(gf, 127, 1))
            down = jnp.where(lane == 0, 0.0, pltpu.roll(gf, 1, 1))
            g3[z, x, 0:128] = up.astype(BF16)
            g3[z, x, 128:256] = gf.astype(BF16)
            g3[z, x, 256:384] = down.astype(BF16)

    upper = zi // 2
    turns = (zi + 1 - 2 * (zi % 2), 2 - upper, 3 - 3 * upper)

    def w_z(to, source):
        return copy(
            wg.at[core, yi, source], wg.at[core, yi, source],
            ws.at[0, to], wr.at[0, source], dev(to * 4 + yi * 2 + xi),
        )

    def w_y(z):
        return copy(wg.at[core, yi, z], wg.at[core, yi, z], ws.at[1, z], wr.at[1, z], dev(y_peer))

    w_c = [
        copy(wg.at[core, row], wg.at[core, row], ws.at[2, 1 + k], wr.at[2, 1 + k], dev(me, other))
        for k, row in enumerate((yi, 1 - yi))
    ]

    def tap(j):
        dz, at = j
        return dz * 3 + (1, 2 - 2 * xi, 2 * xi)[at]

    def product(j, cells, total=None):
        dz = j[0]
        dx = tap(j) - 3 * dz
        for at in range(0, len(cells), 4):
            four = cells[at : at + 4]
            term = lax.dot_general(
                jnp.concatenate([g3[z, x] for z, x in four], axis=1),
                jnp.concatenate([vp[z + dz, dx + x] for z, x in four], axis=1),
                (((1,), (1,)), ((), ())), preferred_element_type=F32,
            )
            total = term if total is None else total + term
        return total

    def own(j):
        first = (0, xi, 1 - xi)[j[1]]
        cells = [(z, first + k) for z in range(4) for k in range(3)]
        held[j[1] - 1, j[0]] = product(j, cells)

    def grad(j):
        if j[1] == 0:
            total = product(j, [(z, x) for z in range(4) for x in range(4)])
        else:
            last_x = (0, 3 - 3 * xi, 3 * xi)[j[1]]
            total = product(j, [(z, last_x) for z in range(4)], held[j[1] - 1, j[0]])
        for h in range(2):
            blocks = total[:, h * 128 : h * 128 + 128].reshape(3, 4, 2, 2, 8, 128)
            for y in range(2):
                for x in range(2):
                    for dy in range(3):
                        first, second = (x, y) if not y_first(j) else (y, x)
                        part[tap(j), h, first, second, :, dy] = blocks[dy, :, y, x]

    def encode(value, bound):
        t = value.reshape(-1, 8, 128) * ((TOP / REACH) / bound)
        a = t * t
        coded = (a * a * (a * t)).reshape(value.shape)
        ends = [bound] if value.shape[0] % 16 else [bound, bound]
        return jnp.concatenate([coded] + ends, axis=0).astype(BF16)

    def decode(coded, count):
        value = coded.astype(F32).reshape(-1, 8, 128)
        bound = value[count]
        value = value[:count]
        size = jnp.exp2(jnp.log2(jnp.abs(value)) * (1.0 / 7.0)) * (bound * (REACH / TOP))
        return jnp.where(value < 0, -size, size), bound

    def stage_a(j):
        i = tap(j)
        return copy(part.at[i, other], ra.at[i], rs_s.at[0, i], rs_r.at[0, i], dev(me, other))

    def y_first(j):
        return j[0] in Y_FIRST[j[1] > 0]

    def path(j):
        return ((xi, x_peer), (yi, y_peer)) if not y_first(j) else ((yi, y_peer), (xi, x_peer))

    def stage_1(j):
        i = tap(j)
        return copy(e1.at[i], r1.at[i], rs_s.at[1, i], rs_r.at[1, i], dev(path(j)[0][1]))

    def stage_2(j):
        i = tap(j)
        return copy(e2.at[i], r2.at[i], rs_s.at[2, i], rs_r.at[2, i], dev(path(j)[1][1]))

    def stage_3(at):
        return [
            copy(e3.at[at, z_to[k]], r3.at[at, k], zs.at[at, k], zr.at[at, k], dev(z_peer[k]))
            for k in range(3)
        ]

    def last(at):
        block = gs.at[core, :, pl.ds(3 * tap((0, at)), 3)]
        return copy(block, block, ls.at[at], lr.at[at], dev(me, other))

    def after_a(j):
        i = tap(j)
        stage_a(j).wait_recv()
        side = path(j)[0][0]
        away = ra[i, 1 - side] + part[i, core, 1 - side]
        e1[i] = encode(away.reshape(192, 128), most[2])
        stage_1(j).start()
        b1[i] = ra[i, side] + part[i, core, side]

    def after_1(j):
        i = tap(j)
        stage_1(j).wait_recv()
        value, bound = decode(r1[i], 24)
        bound = jnp.maximum(bound, most[2])
        scale[i] = bound
        side = path(j)[1][0]
        value = value.reshape(2, 4, 3, 8, 128)
        b1[i] = b1[i] + value
        e2[i] = encode(b1[i, 1 - side].reshape(96, 128), bound)
        stage_2(j).start()

    def after_2(j):
        i = tap(j)
        stage_2(j).wait_recv()
        side = path(j)[1][0]
        value, bound = decode(r2[i], 12)
        scale[i] = jnp.maximum(bound, scale[i])
        b1[i, side] = b1[i, side] + value.reshape(4, 3, 8, 128)

    def to_line(at):
        taps = [tap((dz, at)) for dz in range(3)]
        side = path((0, at))[1][0]
        bound = jnp.maximum(scale[taps[0]], jnp.maximum(scale[taps[1]], scale[taps[2]]))
        for k, c in enumerate(stage_3(at)):
            rows = jnp.concatenate([b1[i, side, z_to[k]] for i in taps], axis=0)
            e3[at, z_to[k]] = encode(rows.reshape(72, 128), bound)
            c.start()

    def from_line(at):
        taps = [tap((dz, at)) for dz in range(3)]
        side = path((0, at))[1][0]
        total = jnp.concatenate([b1[i, side, zi] for i in taps], axis=0)
        for k, c in enumerate(stage_3(at)):
            c.wait_recv()
            total = total + decode(r3[at, k], 9)[0]
        gs[core, :, pl.ds(3 * taps[0], 3)] = total.reshape(3, 3, 8, 128)
        last(at).start()

    def arrange(row):
        for h in range(2):
            for z in range(4):
                pair = [wg[h, row, z, x].astype(F32).reshape(27, 8, 128) for x in range(2)]
                rows = jnp.concatenate(pair, axis=1).astype(BF16).reshape(9, 3, 16, 128)
                for dy in range(3):
                    at = dy * 64 + z * 16
                    w9[row, :, at : at + 16, h * 128 : h * 128 + 128] = rows[:, dy]

    def forward(row, u):
        z, half = u // 2, u % 2
        total = None
        for dz in range(3):
            for dx in range(3):
                at = dx + 2 * half
                cells = jnp.concatenate([vp[z + dz, at], vp[z + dz, at + 1]], axis=1)
                term = jnp.dot(w9[row, dz * 3 + dx], cells, preferred_element_type=F32)
                total = term if total is None else total + term
        edge = lane[0:64]
        for x in range(2):
            cols = slice(x * 128, x * 128 + 128)
            low = jnp.where(edge == 0, 0.0, pltpu.roll(total[0:64, cols], 1, 1))
            high = jnp.where(edge == 127, 0.0, pltpu.roll(total[128:192, cols], 127, 1))
            value = low + total[64:128, cols] + high + bias[:, row].reshape(64, 128)
            for part_z in range(4):
                at = (part_z * 32 + row * 16) * 16 + 4 * z + x + 2 * half
                wide[pl.ds(at, 16, stride=16), :] = value[part_z * 16 : part_z * 16 + 16]

    edge_slot = 4 - 3 * core
    near_corner = copy(vp.at[edge_slot, near_slot], vp.at[send_slot, near_slot], hs.at[3], hr.at[3], dev(me, other))
    far_corner = copy(vp.at[edge_slot, far_slot], vp.at[send_slot, far_slot], hs.at[4], hr.at[4], dev(me, other))

    def near_edge():
        near[0].wait_recv()
        near_corner.start()

    def near_rim():
        near[1].wait_recv()
        near_corner.wait_recv()

    def far_edge():
        @pl.when(has_far)
        def _():
            far[0].wait_recv()
            far_corner.start()

    def far_rim():
        @pl.when(has_far)
        def _():
            far[1].wait_recv()
            far_corner.wait_recv()

    def chunk(j):
        grad(j)
        stage_a(j).start()

    def spread(k):
        z = turns[k]
        w_z(z, z).wait_recv()
        w_y(z).start()

    mid, near_1, far_1 = [[(dz, at) for dz in (1, 0, 2)] for at in (0, 1, 2)]
    inner.wait_recv()
    chunk(mid[0])
    share.wait_recv()
    most[2] = jnp.maximum(most[0], most[1])
    w_x.wait_recv()
    for z in turns:
        w_z(z, zi).start()
    w_y(zi).start()
    chunk(mid[1])
    after_a(mid[0])
    chunk(mid[2])
    after_a(mid[1])
    far_edge()
    after_a(mid[2])
    for j in far_1:
        own(j)
    far_rim()
    for j in far_1:
        chunk(j)
    after_1(mid[0])
    after_1(mid[1])
    after_a(far_1[0])
    after_a(far_1[1])
    after_1(mid[2])
    after_a(far_1[2])
    spread(0)
    near_edge()
    for j in near_1:
        own(j)
    spread(1)
    near_rim()
    for j in near_1:
        chunk(j)
    after_2(mid[0])
    for j in near_1:
        after_a(j)
    spread(2)
    w_c[0].start()
    after_1(near_1[0])
    after_2(mid[1])
    after_1(near_1[1])
    after_2(mid[2])
    to_line(0)
    after_1(near_1[2])
    w_c[0].wait_recv()
    arrange(yi)
    after_1(far_1[0])
    forward(yi, 0)
    after_1(far_1[1])
    forward(yi, 1)
    after_1(far_1[2])
    after_2(near_1[0])
    forward(yi, 2)
    after_2(near_1[1])
    forward(yi, 3)
    after_2(near_1[2])
    to_line(1)
    for z in range(4):
        w_y(z).wait_recv()
    w_c[1].start()
    forward(yi, 4)
    after_2(far_1[0])
    forward(yi, 5)
    after_2(far_1[1])
    forward(yi, 6)
    after_2(far_1[2])
    to_line(2)
    forward(yi, 7)
    w_c[1].wait_recv()
    arrange(1 - yi)
    from_line(0)
    for u in range(4):
        forward(1 - yi, u)
    from_line(1)
    forward(1 - yi, 4)
    forward(1 - yi, 5)
    from_line(2)
    forward(1 - yi, 6)
    forward(1 - yi, 7)
    out_ref[...] = wide[...].astype(BF16)
    for c in near:
        c.wait_send()
    near_corner.wait_send()
    share.wait_send()

    @pl.when(has_far)
    def _():
        for c in far:
            c.wait_send()
        far_corner.wait_send()

    inner.wait_send()
    for z in turns:
        w_z(z, zi).wait_send()
    for c in [w_y(z) for z in range(4)] + w_c + [w_x]:
        c.wait_send()
    for j in mid + near_1 + far_1:
        stage_a(j).wait_send()
        stage_1(j).wait_send()
        stage_2(j).wait_send()
    for at in range(3):
        for c in stage_3(at):
            c.wait_send()
        last(at).wait()
    for h in range(2):
        gw_ref[:, :, h * 128 : h * 128 + 128] = gs[h].reshape(27, 8, 128)


def fused_body(volume, weights, bias, grad_out):
    v = volume.reshape(4096, 128)
    g = grad_out.reshape(2048, 128)
    w = weights.transpose(1, 0, 2).reshape(216, 256)
    b = bias.reshape(1, 128)
    vmem = pl.BlockSpec(memory_space=pltpu.VMEM)
    hold = lambda a: pltpu.with_memory_space_constraint(a, pltpu.HBM)
    hbm = pl.BlockSpec(memory_space=pltpu.HBM)
    dma = pltpu.SemaphoreType.DMA
    out, gw = pl.pallas_call(
        fused_kernel,
        out_shape=(
            jax.ShapeDtypeStruct((2048, 128), BF16),
            jax.ShapeDtypeStruct((27, 8, 256), F32),
        ),
        in_specs=[hbm] * 4,
        out_specs=(vmem, vmem),
        scratch_shapes=[
            pltpu.VMEM((6, 6, 256, 128), BF16),
            pltpu.VMEM((4, 4, 384, 128), BF16),
            pltpu.VMEM((2, 2, 4, 2, 216, 128), BF16),
            pltpu.VMEM((2, 9, 192, 256), BF16),
            pltpu.VMEM((9, 2, 2, 2, 4, 3, 8, 128), F32),
            pltpu.VMEM((9, 2, 2, 4, 3, 8, 128), F32),
            pltpu.VMEM((9, 208, 128), BF16),
            pltpu.VMEM((9, 208, 128), BF16),
            pltpu.VMEM((9, 2, 4, 3, 8, 128), F32),
            pltpu.VMEM((9, 112, 128), BF16),
            pltpu.VMEM((9, 112, 128), BF16),
            pltpu.VMEM((3, 4, 80, 128), BF16),
            pltpu.VMEM((3, 3, 80, 128), BF16),
            pltpu.VMEM((2, 3, 9, 8, 128), F32),
            pltpu.VMEM((3, 8, 128), F32),
            pltpu.VMEM((9, 8, 128), F32),
            dma((8,)), dma((8,)), dma((3, 4)), dma((3, 4)),
            dma((3, 9)), dma((3, 9)), dma((3, 3)), dma((3, 3)),
            dma, dma,
            pltpu.VMEM((4, 2, 16, 128), F32),
            pltpu.VMEM((2048, 128), F32),
            pltpu.VMEM((4096, 128), BF16),
            pltpu.VMEM((2048, 128), BF16),
            pltpu.VMEM((1, 128), F32),
            pltpu.VMEM((4096, 128), F32),
            dma((4,)),
            pltpu.VMEM((2, 3, 384, 256), F32),
            dma((3,)), dma((3,)),
        ],
        compiler_params=pltpu.CompilerParams(
            collective_id=0, has_side_effects=True, vmem_limit_bytes=48 << 20
        ),
    )(hold(v), hold(w), hold(b), hold(g))
    output = out.reshape(128, 4, 4, 128)
    grad_w = gw.transpose(1, 0, 2)
    return (output, grad_w)


def solution(mesh):
    in_specs = (
        P(None, "depth", "filt", None),
        P("filt", None, None),
        P(),
        P(None, "depth", "filt", None),
    )
    out_specs = (P(None, "depth", "filt", None), P("filt", None, None))
    small = mesh.shape["filt"] == 16 and mesh.shape["depth"] == 2

    def body(volume, weights, bias, grad_out):
        shapes = (volume.shape, weights.shape, grad_out.shape)
        if small and shapes == ((256, 4, 4, 128), (8, 27, 256), (128, 4, 4, 128)):
            return fused_body(volume, weights, bias, grad_out)
        return general_body(volume, weights, bias, grad_out)

    return jax.shard_map(body, mesh=mesh, in_specs=in_specs, out_specs=out_specs, check_vma=False)
```

```python
import jax
import jax.numpy as jnp
from jax import lax
from jax.experimental import pallas as pl
from jax.experimental.pallas import tpu as pltpu
from jax.sharding import PartitionSpec as P

F32 = jnp.float32
BF16 = jnp.bfloat16
Y_FIRST = ((0, 1, 2), ())
MESH = pl.DeviceIdType.MESH


def padded_2(block, sides, width):
    for axis, dim in sides:
        count = lax.axis_size(axis)
        forward = [(i, i + 1) for i in range(count - 1)]
        backward = [(target, source) for source, target in forward]
        low = lax.ppermute(
            lax.slice_in_dim(block, block.shape[dim] - width, None, axis=dim), axis, forward
        )
        high = lax.ppermute(lax.slice_in_dim(block, 0, width, axis=dim), axis, backward)
        block = jnp.concatenate([low, block, high], axis=dim)
    return block


def general_body(volume, weights, bias, grad_out):
    channels = volume.shape[0]
    rimmed = padded_2(volume, (("filt", 2), ("depth", 1)), 1)
    padded = jnp.pad(rimmed, ((0, 0), (0, 0), (0, 0), (1, 1)))
    stacked = padded[None]
    per_channel = padded[:, None]
    piece = lax.all_gather(weights, "filt", axis=0, tiled=True)
    count = piece.shape[0]
    kernel = piece.reshape(count, 3, 3, 3, channels)
    result = lax.conv_general_dilated(
        stacked,
        kernel,
        (1, 1, 1),
        "VALID",
        dimension_numbers=("NCDHW", "ODHWI", "NCDHW"),
        preferred_element_type=jnp.float32,
    )
    output = (result[0] + bias[:, None, None, None]).astype(jnp.bfloat16)
    all_filters = grad_out.shape[0]
    taps = lax.conv_general_dilated(
        per_channel,
        grad_out[:, None],
        (1, 1, 1),
        "VALID",
        dimension_numbers=("NCDHW", "OIDHW", "CDHWN"),
        preferred_element_type=jnp.float32,
    )
    term = taps.reshape(all_filters, 27, channels)
    summed = lax.psum(term, "depth")
    grad_w = lax.psum_scatter(summed, "filt", scatter_dimension=0, tiled=True)
    return (output, grad_w)


REACH = 6.0 * 65536
TOP = 2.0 ** 17.5


def fused_kernel(
    v_hbm, w_hbm, b_hbm, g_hbm,
    out_ref, gw_ref,
    vp, g3, wg, w9, part, ra, e1, r1, b1, e2, r2, e3, r3, gs, most, scale,
    hs, hr, ws, wr, rs_s, rs_r, zs, zr, ms, mr, bias, wide, v_in, g_in, b_in, v_wide, loads, held, ls, lr,
):
    me = lax.axis_index("filt")
    core = lax.axis_index("depth")
    other = 1 - core
    xi = me % 2
    yi = (me // 2) % 2
    zi = me // 4
    x_peer = me + 1 - 2 * xi
    y_peer = me + 2 - 4 * yi
    z_to = [(zi + k) % 4 for k in (1, 2, 3)]
    z_peer = [t * 4 + yi * 2 + xi for t in z_to]
    far_peer = me - 1 + 2 * xi
    has_far = jnp.logical_and(me > 0, me < 15)
    near_slot, far_slot = 5 - 5 * xi, 5 * xi

    def dev(filt, depth=None):
        return {"filt": filt, "depth": core if depth is None else depth}

    def copy(src, dst, s_sem, r_sem, device):
        return pltpu.make_async_remote_copy(
            src_ref=src, dst_ref=dst, send_sem=s_sem, recv_sem=r_sem,
            device_id=device, device_id_type=MESH,
        )

    v_load = pltpu.make_async_copy(v_hbm, v_in, loads.at[0])
    g_load = pltpu.make_async_copy(g_hbm, g_in, loads.at[1])
    b_load = pltpu.make_async_copy(b_hbm, b_in, loads.at[2])
    half = pl.ds(pl.multiple_of(core * 128, 128), 128)
    w_load = pltpu.make_async_copy(w_hbm.at[:, half], wg.at[core, yi, zi, xi], loads.at[3])
    v_load.start()
    w_load.start()
    g_load.start()
    b_load.start()
    barrier = pltpu.get_barrier_semaphore()

    def greet(device):
        pl.semaphore_signal(barrier, inc=1, device_id=device, device_id_type=MESH)

    greet(dev(me, other))
    greet(dev(x_peer))
    greet(dev(y_peer))
    for p in z_peer:
        greet(dev(p))

    @pl.when(has_far)
    def _():
        greet(dev(far_peer))

    def place(z, x):
        vp[z + 1, x + 1] = v_wide[pl.ds(4 * z + x, 256, stride=16), :].astype(BF16)

    v_load.wait()
    v_wide[...] = v_in[...].astype(F32)
    for z in range(4):
        place(z, 0)
        place(z, 3)
    pl.semaphore_wait(barrier, 5 + jnp.minimum(me, 1) + jnp.minimum(15 - me, 1))

    w_x = copy(wg.at[core, yi, zi, xi], wg.at[core, yi, zi, xi], ws.at[2, 0], wr.at[2, 0], dev(x_peer))
    w_load.wait()
    w_x.start()

    my_edge = 3 - 3 * core
    planes = (pl.ds(my_edge + 1, 1), pl.ds(1 + core, 3))
    near = [
        copy(vp.at[p, 4 - 3 * xi], vp.at[p, 5 * xi], hs.at[k], hr.at[k], dev(x_peer))
        for k, p in enumerate(planes)
    ]
    far = [
        copy(vp.at[p, 1 + 3 * xi], vp.at[p, 5 - 5 * xi], hs.at[6 + k], hr.at[6 + k], dev(far_peer))
        for k, p in enumerate(planes)
    ]

    @pl.when(has_far)
    def _():
        for c in far:
            c.start()

    for c in near:
        c.start()
    for z in range(4):
        place(z, 1)
        place(z, 2)
    send_slot = 5 - 5 * other
    inner = copy(vp.at[my_edge + 1, 1:5], vp.at[send_slot, 1:5], hs.at[2], hr.at[2], dev(me, other))
    inner.start()
    g_load.wait()
    wide[...] = g_in[...].astype(F32)
    top = jnp.max(jnp.abs(wide[...]).reshape(256, 8, 128), axis=0)
    top = jnp.max(jnp.max(top, axis=0, keepdims=True), axis=1, keepdims=True)
    most[0] = jnp.broadcast_to(jnp.maximum(top, 2.0 ** -100), (8, 128))
    share = copy(most.at[0], most.at[1], ms, mr, dev(me, other))
    share.start()
    b_load.wait()
    bias[...] = jnp.broadcast_to(b_in[...], (128, 128)).T.reshape(4, 2, 16, 128)
    empty = 5 - 5 * (1 - core)
    vp[empty] = jnp.zeros((6, 256, 128), BF16)

    @pl.when(jnp.logical_not(has_far))
    def _():
        vp[1:5, far_slot] = jnp.zeros((4, 256, 128), BF16)
        vp[send_slot, far_slot] = jnp.zeros((256, 128), BF16)

    lane = lax.broadcasted_iota(jnp.int32, (128, 128), 1)
    for z in range(4):
        for x in range(4):
            gf = wide[pl.ds(4 * z + x, 128, stride=16), :]
            up = jnp.where(lane == 127, 0.0, pltpu.roll(gf, 127, 1))
            down = jnp.where(lane == 0, 0.0, pltpu.roll(gf, 1, 1))
            g3[z, x, 0:128] = up.astype(BF16)
            g3[z, x, 128:256] = gf.astype(BF16)
            g3[z, x, 256:384] = down.astype(BF16)

    upper = zi // 2
    turns = (zi + 1 - 2 * (zi % 2), 2 - upper, 3 - 3 * upper)

    def w_z(to, source):
        return copy(
            wg.at[core, yi, source], wg.at[core, yi, source],
            ws.at[0, to], wr.at[0, source], dev(to * 4 + yi * 2 + xi),
        )

    def w_y(z):
        return copy(wg.at[core, yi, z], wg.at[core, yi, z], ws.at[1, z], wr.at[1, z], dev(y_peer))

    w_c = [
        copy(wg.at[core, row], wg.at[core, row], ws.at[2, 1 + k], wr.at[2, 1 + k], dev(me, other))
        for k, row in enumerate((yi, 1 - yi))
    ]

    def tap(j):
        dz, at = j
        return dz * 3 + (1, 2 - 2 * xi, 2 * xi)[at]

    def product(j, cells, total=None):
        dz = j[0]
        dx = tap(j) - 3 * dz
        for at in range(0, len(cells), 4):
            four = cells[at : at + 4]
            term = lax.dot_general(
                jnp.concatenate([g3[z, x] for z, x in four], axis=1),
                jnp.concatenate([vp[z + dz, dx + x] for z, x in four], axis=1),
                (((1,), (1,)), ((), ())), preferred_element_type=F32,
            )
            total = term if total is None else total + term
        return total

    def own(j):
        first = (0, xi, 1 - xi)[j[1]]
        cells = [(z, first + k) for z in range(4) for k in range(3)]
        held[j[1] - 1, j[0]] = product(j, cells)

    def grad(j):
        if j[1] == 0:
            total = product(j, [(z, x) for z in range(4) for x in range(4)])
        else:
            last_x = (0, 3 - 3 * xi, 3 * xi)[j[1]]
            total = product(j, [(z, last_x) for z in range(4)], held[j[1] - 1, j[0]])
        for h in range(2):
            blocks = total[:, h * 128 : h * 128 + 128].reshape(3, 4, 2, 2, 8, 128)
            for y in range(2):
                for x in range(2):
                    for dy in range(3):
                        first, second = (x, y) if not y_first(j) else (y, x)
                        part[tap(j), h, first, second, :, dy] = blocks[dy, :, y, x]

    def encode(value, bound):
        t = value.reshape(-1, 8, 128) * ((TOP / REACH) / bound)
        a = t * t
        coded = (a * a * (a * t)).reshape(value.shape)
        ends = [bound] if value.shape[0] % 16 else [bound, bound]
        return jnp.concatenate([coded] + ends, axis=0).astype(BF16)

    def decode(coded, count):
        value = coded.astype(F32).reshape(-1, 8, 128)
        bound = value[count]
        value = value[:count]
        size = jnp.exp2(jnp.log2(jnp.abs(value)) * (1.0 / 7.0)) * (bound * (REACH / TOP))
        return jnp.where(value < 0, -size, size), bound

    def stage_a(j):
        i = tap(j)
        return copy(part.at[i, other], ra.at[i], rs_s.at[0, i], rs_r.at[0, i], dev(me, other))

    def y_first(j):
        return j[0] in Y_FIRST[j[1] > 0]

    def path(j):
        return ((xi, x_peer), (yi, y_peer)) if not y_first(j) else ((yi, y_peer), (xi, x_peer))

    def stage_1(j):
        i = tap(j)
        return copy(e1.at[i], r1.at[i], rs_s.at[1, i], rs_r.at[1, i], dev(path(j)[0][1]))

    def stage_2(j):
        i = tap(j)
        return copy(e2.at[i], r2.at[i], rs_s.at[2, i], rs_r.at[2, i], dev(path(j)[1][1]))

    def stage_3(at):
        return [
            copy(e3.at[at, z_to[k]], r3.at[at, k], zs.at[at, k], zr.at[at, k], dev(z_peer[k]))
            for k in range(3)
        ]

    def last(at):
        block = gs.at[core, :, pl.ds(3 * tap((0, at)), 3)]
        return copy(block, block, ls.at[at], lr.at[at], dev(me, other))

    def after_a(j):
        i = tap(j)
        stage_a(j).wait_recv()
        side = path(j)[0][0]
        away = ra[i, 1 - side] + part[i, core, 1 - side]
        e1[i] = encode(away.reshape(192, 128), most[2])
        stage_1(j).start()
        b1[i] = ra[i, side] + part[i, core, side]

    def after_1(j):
        i = tap(j)
        stage_1(j).wait_recv()
        value, bound = decode(r1[i], 24)
        bound = jnp.maximum(bound, most[2])
        scale[i] = bound
        side = path(j)[1][0]
        value = value.reshape(2, 4, 3, 8, 128)
        b1[i] = b1[i] + value
        e2[i] = encode(b1[i, 1 - side].reshape(96, 128), bound)
        stage_2(j).start()

    def after_2(j):
        i = tap(j)
        stage_2(j).wait_recv()
        side = path(j)[1][0]
        value, bound = decode(r2[i], 12)
        scale[i] = jnp.maximum(bound, scale[i])
        b1[i, side] = b1[i, side] + value.reshape(4, 3, 8, 128)

    def to_line(at):
        taps = [tap((dz, at)) for dz in range(3)]
        side = path((0, at))[1][0]
        bound = jnp.maximum(scale[taps[0]], jnp.maximum(scale[taps[1]], scale[taps[2]]))
        for k, c in enumerate(stage_3(at)):
            rows = jnp.concatenate([b1[i, side, z_to[k]] for i in taps], axis=0)
            e3[at, z_to[k]] = encode(rows.reshape(72, 128), bound)
            c.start()

    def from_line(at):
        taps = [tap((dz, at)) for dz in range(3)]
        side = path((0, at))[1][0]
        total = jnp.concatenate([b1[i, side, zi] for i in taps], axis=0)
        for k, c in enumerate(stage_3(at)):
            c.wait_recv()
            total = total + decode(r3[at, k], 9)[0]
        gs[core, :, pl.ds(3 * taps[0], 3)] = total.reshape(3, 3, 8, 128)
        last(at).start()

    def arrange(row):
        for h in range(2):
            for z in range(4):
                pair = [wg[h, row, z, x].astype(F32).reshape(27, 8, 128) for x in range(2)]
                rows = jnp.concatenate(pair, axis=1).astype(BF16).reshape(9, 3, 16, 128)
                for dy in range(3):
                    at = dy * 64 + z * 16
                    w9[row, :, at : at + 16, h * 128 : h * 128 + 128] = rows[:, dy]

    def forward(row, u):
        z, half = u // 2, u % 2
        total = None
        for dz in range(3):
            for dx in range(3):
                at = dx + 2 * half
                cells = jnp.concatenate([vp[z + dz, at], vp[z + dz, at + 1]], axis=1)
                term = jnp.dot(w9[row, dz * 3 + dx], cells, preferred_element_type=F32)
                total = term if total is None else total + term
        edge = lane[0:64]
        for x in range(2):
            cols = slice(x * 128, x * 128 + 128)
            low = jnp.where(edge == 0, 0.0, pltpu.roll(total[0:64, cols], 1, 1))
            high = jnp.where(edge == 127, 0.0, pltpu.roll(total[128:192, cols], 127, 1))
            value = low + total[64:128, cols] + high + bias[:, row].reshape(64, 128)
            for part_z in range(4):
                at = (part_z * 32 + row * 16) * 16 + 4 * z + x + 2 * half
                wide[pl.ds(at, 16, stride=16), :] = value[part_z * 16 : part_z * 16 + 16]

    edge_slot = 4 - 3 * core
    near_corner = copy(vp.at[edge_slot, near_slot], vp.at[send_slot, near_slot], hs.at[3], hr.at[3], dev(me, other))
    far_corner = copy(vp.at[edge_slot, far_slot], vp.at[send_slot, far_slot], hs.at[4], hr.at[4], dev(me, other))

    def near_edge():
        near[0].wait_recv()
        near_corner.start()

    def near_rim():
        near[1].wait_recv()
        near_corner.wait_recv()

    def far_edge():
        @pl.when(has_far)
        def _():
            far[0].wait_recv()
            far_corner.start()

    def far_rim():
        @pl.when(has_far)
        def _():
            far[1].wait_recv()
            far_corner.wait_recv()

    def chunk(j):
        grad(j)
        stage_a(j).start()

    def spread(k):
        z = turns[k]
        w_z(z, z).wait_recv()
        w_y(z).start()

    mid, near_1, far_1 = [[(dz, at) for dz in (1, 0, 2)] for at in (0, 1, 2)]
    inner.wait_recv()
    chunk(mid[0])
    share.wait_recv()
    most[2] = jnp.maximum(most[0], most[1])
    w_x.wait_recv()
    for z in turns:
        w_z(z, zi).start()
    w_y(zi).start()
    chunk(mid[1])
    after_a(mid[0])
    chunk(mid[2])
    after_a(mid[1])
    far_edge()
    after_a(mid[2])
    for j in far_1:
        own(j)
    spread(0)
    far_rim()
    for j in far_1:
        chunk(j)
    after_1(mid[0])
    after_1(mid[1])
    after_a(far_1[0])
    after_a(far_1[1])
    after_1(mid[2])
    after_a(far_1[2])
    near_edge()
    for j in near_1:
        own(j)
    spread(1)
    near_rim()
    for j in near_1:
        chunk(j)
    after_2(mid[0])
    for j in near_1:
        after_a(j)
    spread(2)
    w_c[0].start()
    after_1(near_1[0])
    after_2(mid[1])
    after_1(near_1[1])
    after_2(mid[2])
    to_line(0)
    after_1(near_1[2])
    w_c[0].wait_recv()
    arrange(yi)
    after_1(far_1[0])
    forward(yi, 0)
    after_1(far_1[1])
    forward(yi, 1)
    after_1(far_1[2])
    for z in range(4):
        w_y(z).wait_recv()
    w_c[1].start()
    after_2(near_1[0])
    forward(yi, 2)
    after_2(near_1[1])
    forward(yi, 3)
    after_2(near_1[2])
    to_line(1)
    forward(yi, 4)
    after_2(far_1[0])
    forward(yi, 5)
    after_2(far_1[1])
    forward(yi, 6)
    after_2(far_1[2])
    to_line(2)
    forward(yi, 7)
    w_c[1].wait_recv()
    arrange(1 - yi)
    from_line(0)
    for u in range(4):
        forward(1 - yi, u)
    from_line(1)
    forward(1 - yi, 4)
    forward(1 - yi, 5)
    from_line(2)
    forward(1 - yi, 6)
    forward(1 - yi, 7)
    out_ref[...] = wide[...].astype(BF16)
    for c in near:
        c.wait_send()
    near_corner.wait_send()
    share.wait_send()

    @pl.when(has_far)
    def _():
        for c in far:
            c.wait_send()
        far_corner.wait_send()

    inner.wait_send()
    for z in turns:
        w_z(z, zi).wait_send()
    for c in [w_y(z) for z in range(4)] + w_c + [w_x]:
        c.wait_send()
    for j in mid + near_1 + far_1:
        stage_a(j).wait_send()
        stage_1(j).wait_send()
        stage_2(j).wait_send()
    for at in range(3):
        for c in stage_3(at):
            c.wait_send()
        last(at).wait()
    for h in range(2):
        gw_ref[:, :, h * 128 : h * 128 + 128] = gs[h].reshape(27, 8, 128)


def fused_body(volume, weights, bias, grad_out):
    v = volume.reshape(4096, 128)
    g = grad_out.reshape(2048, 128)
    w = weights.transpose(1, 0, 2).reshape(216, 256)
    b = bias.reshape(1, 128)
    vmem = pl.BlockSpec(memory_space=pltpu.VMEM)
    hold = lambda a: pltpu.with_memory_space_constraint(a, pltpu.HBM)
    hbm = pl.BlockSpec(memory_space=pltpu.HBM)
    dma = pltpu.SemaphoreType.DMA
    out, gw = pl.pallas_call(
        fused_kernel,
        out_shape=(
            jax.ShapeDtypeStruct((2048, 128), BF16),
            jax.ShapeDtypeStruct((27, 8, 256), F32),
        ),
        in_specs=[hbm] * 4,
        out_specs=(vmem, vmem),
        scratch_shapes=[
            pltpu.VMEM((6, 6, 256, 128), BF16),
            pltpu.VMEM((4, 4, 384, 128), BF16),
            pltpu.VMEM((2, 2, 4, 2, 216, 128), BF16),
            pltpu.VMEM((2, 9, 192, 256), BF16),
            pltpu.VMEM((9, 2, 2, 2, 4, 3, 8, 128), F32),
            pltpu.VMEM((9, 2, 2, 4, 3, 8, 128), F32),
            pltpu.VMEM((9, 208, 128), BF16),
            pltpu.VMEM((9, 208, 128), BF16),
            pltpu.VMEM((9, 2, 4, 3, 8, 128), F32),
            pltpu.VMEM((9, 112, 128), BF16),
            pltpu.VMEM((9, 112, 128), BF16),
            pltpu.VMEM((3, 4, 80, 128), BF16),
            pltpu.VMEM((3, 3, 80, 128), BF16),
            pltpu.VMEM((2, 3, 9, 8, 128), F32),
            pltpu.VMEM((3, 8, 128), F32),
            pltpu.VMEM((9, 8, 128), F32),
            dma((8,)), dma((8,)), dma((3, 4)), dma((3, 4)),
            dma((3, 9)), dma((3, 9)), dma((3, 3)), dma((3, 3)),
            dma, dma,
            pltpu.VMEM((4, 2, 16, 128), F32),
            pltpu.VMEM((2048, 128), F32),
            pltpu.VMEM((4096, 128), BF16),
            pltpu.VMEM((2048, 128), BF16),
            pltpu.VMEM((1, 128), F32),
            pltpu.VMEM((4096, 128), F32),
            dma((4,)),
            pltpu.VMEM((2, 3, 384, 256), F32),
            dma((3,)), dma((3,)),
        ],
        compiler_params=pltpu.CompilerParams(
            collective_id=0, has_side_effects=True, vmem_limit_bytes=48 << 20
        ),
    )(hold(v), hold(w), hold(b), hold(g))
    output = out.reshape(128, 4, 4, 128)
    grad_w = gw.transpose(1, 0, 2)
    return (output, grad_w)


def solution(mesh):
    in_specs = (
        P(None, "depth", "filt", None),
        P("filt", None, None),
        P(),
        P(None, "depth", "filt", None),
    )
    out_specs = (P(None, "depth", "filt", None), P("filt", None, None))
    small = mesh.shape["filt"] == 16 and mesh.shape["depth"] == 2

    def body(volume, weights, bias, grad_out):
        shapes = (volume.shape, weights.shape, grad_out.shape)
        if small and shapes == ((256, 4, 4, 128), (8, 27, 256), (128, 4, 4, 128)):
            return fused_body(volume, weights, bias, grad_out)
        return general_body(volume, weights, bias, grad_out)

    return jax.shard_map(body, mesh=mesh, in_specs=in_specs, out_specs=out_specs, check_vma=False)
```

```python
import jax
import jax.numpy as jnp
from jax import lax
from jax.experimental import pallas as pl
from jax.experimental.pallas import tpu as pltpu
from jax.sharding import PartitionSpec as P

F32 = jnp.float32
BF16 = jnp.bfloat16
Y_FIRST = ((0, 1, 2), ())
MESH = pl.DeviceIdType.MESH


def padded_2(block, sides, width):
    for axis, dim in sides:
        count = lax.axis_size(axis)
        forward = [(i, i + 1) for i in range(count - 1)]
        backward = [(target, source) for source, target in forward]
        low = lax.ppermute(
            lax.slice_in_dim(block, block.shape[dim] - width, None, axis=dim), axis, forward
        )
        high = lax.ppermute(lax.slice_in_dim(block, 0, width, axis=dim), axis, backward)
        block = jnp.concatenate([low, block, high], axis=dim)
    return block


def general_body(volume, weights, bias, grad_out):
    channels = volume.shape[0]
    rimmed = padded_2(volume, (("filt", 2), ("depth", 1)), 1)
    padded = jnp.pad(rimmed, ((0, 0), (0, 0), (0, 0), (1, 1)))
    stacked = padded[None]
    per_channel = padded[:, None]
    piece = lax.all_gather(weights, "filt", axis=0, tiled=True)
    count = piece.shape[0]
    kernel = piece.reshape(count, 3, 3, 3, channels)
    result = lax.conv_general_dilated(
        stacked,
        kernel,
        (1, 1, 1),
        "VALID",
        dimension_numbers=("NCDHW", "ODHWI", "NCDHW"),
        preferred_element_type=jnp.float32,
    )
    output = (result[0] + bias[:, None, None, None]).astype(jnp.bfloat16)
    all_filters = grad_out.shape[0]
    taps = lax.conv_general_dilated(
        per_channel,
        grad_out[:, None],
        (1, 1, 1),
        "VALID",
        dimension_numbers=("NCDHW", "OIDHW", "CDHWN"),
        preferred_element_type=jnp.float32,
    )
    term = taps.reshape(all_filters, 27, channels)
    summed = lax.psum(term, "depth")
    grad_w = lax.psum_scatter(summed, "filt", scatter_dimension=0, tiled=True)
    return (output, grad_w)


REACH = 6.0 * 65536
TOP = 2.0 ** 17.5


def fused_kernel(
    v_hbm, w_hbm, b_hbm, g_hbm,
    out_ref, gw_ref,
    vp, g3, wg, w9, part, ra, e1, r1, b1, e2, r2, e3, r3, gs, most, scale,
    hs, hr, ws, wr, rs_s, rs_r, zs, zr, ms, mr, bias, wide, v_in, g_in, b_in, v_wide, loads, held, ls, lr,
):
    me = lax.axis_index("filt")
    core = lax.axis_index("depth")
    other = 1 - core
    xi = me % 2
    yi = (me // 2) % 2
    zi = me // 4
    x_peer = me + 1 - 2 * xi
    y_peer = me + 2 - 4 * yi
    z_to = [(zi + k) % 4 for k in (1, 2, 3)]
    z_peer = [t * 4 + yi * 2 + xi for t in z_to]
    far_peer = me - 1 + 2 * xi
    has_far = jnp.logical_and(me > 0, me < 15)
    near_slot, far_slot = 5 - 5 * xi, 5 * xi

    def dev(filt, depth=None):
        return {"filt": filt, "depth": core if depth is None else depth}

    def copy(src, dst, s_sem, r_sem, device):
        return pltpu.make_async_remote_copy(
            src_ref=src, dst_ref=dst, send_sem=s_sem, recv_sem=r_sem,
            device_id=device, device_id_type=MESH,
        )

    v_load = pltpu.make_async_copy(v_hbm, v_in, loads.at[0])
    g_load = pltpu.make_async_copy(g_hbm, g_in, loads.at[1])
    b_load = pltpu.make_async_copy(b_hbm, b_in, loads.at[2])
    half = pl.ds(pl.multiple_of(core * 128, 128), 128)
    w_load = pltpu.make_async_copy(w_hbm.at[:, half], wg.at[core, yi, zi, xi], loads.at[3])
    v_load.start()
    w_load.start()
    g_load.start()
    b_load.start()
    barrier = pltpu.get_barrier_semaphore()

    def greet(device):
        pl.semaphore_signal(barrier, inc=1, device_id=device, device_id_type=MESH)

    greet(dev(me, other))
    greet(dev(x_peer))
    greet(dev(y_peer))
    for p in z_peer:
        greet(dev(p))

    @pl.when(has_far)
    def _():
        greet(dev(far_peer))

    def place(z, x):
        vp[z + 1, x + 1] = v_wide[pl.ds(4 * z + x, 256, stride=16), :].astype(BF16)

    v_load.wait()
    v_wide[...] = v_in[...].astype(F32)
    for z in range(4):
        place(z, 0)
        place(z, 3)
    pl.semaphore_wait(barrier, 5 + jnp.minimum(me, 1) + jnp.minimum(15 - me, 1))

    w_x = copy(wg.at[core, yi, zi, xi], wg.at[core, yi, zi, xi], ws.at[2, 0], wr.at[2, 0], dev(x_peer))
    w_load.wait()
    w_x.start()

    my_edge = 3 - 3 * core
    planes = (pl.ds(my_edge + 1, 1), pl.ds(1 + core, 3))
    near = [
        copy(vp.at[p, 4 - 3 * xi], vp.at[p, 5 * xi], hs.at[k], hr.at[k], dev(x_peer))
        for k, p in enumerate(planes)
    ]
    far = [
        copy(vp.at[p, 1 + 3 * xi], vp.at[p, 5 - 5 * xi], hs.at[6 + k], hr.at[6 + k], dev(far_peer))
        for k, p in enumerate(planes)
    ]

    @pl.when(has_far)
    def _():
        for c in far:
            c.start()

    for c in near:
        c.start()
    for z in range(4):
        place(z, 1)
        place(z, 2)
    send_slot = 5 - 5 * other
    inner = copy(vp.at[my_edge + 1, 1:5], vp.at[send_slot, 1:5], hs.at[2], hr.at[2], dev(me, other))
    inner.start()
    g_load.wait()
    wide[...] = g_in[...].astype(F32)
    top = jnp.max(jnp.abs(wide[...]).reshape(256, 8, 128), axis=0)
    top = jnp.max(jnp.max(top, axis=0, keepdims=True), axis=1, keepdims=True)
    most[0] = jnp.broadcast_to(jnp.maximum(top, 2.0 ** -100), (8, 128))
    share = copy(most.at[0], most.at[1], ms, mr, dev(me, other))
    share.start()
    b_load.wait()
    bias[...] = jnp.broadcast_to(b_in[...], (128, 128)).T.reshape(4, 2, 16, 128)
    empty = 5 - 5 * (1 - core)
    vp[empty] = jnp.zeros((6, 256, 128), BF16)

    @pl.when(jnp.logical_not(has_far))
    def _():
        vp[1:5, far_slot] = jnp.zeros((4, 256, 128), BF16)
        vp[send_slot, far_slot] = jnp.zeros((256, 128), BF16)

    lane = lax.broadcasted_iota(jnp.int32, (128, 128), 1)
    for z in range(4):
        for x in range(4):
            gf = wide[pl.ds(4 * z + x, 128, stride=16), :]
            up = jnp.where(lane == 127, 0.0, pltpu.roll(gf, 127, 1))
            down = jnp.where(lane == 0, 0.0, pltpu.roll(gf, 1, 1))
            g3[z, x, 0:128] = up.astype(BF16)
            g3[z, x, 128:256] = gf.astype(BF16)
            g3[z, x, 256:384] = down.astype(BF16)

    upper = zi // 2
    turns = (zi + 1 - 2 * (zi % 2), 2 - upper, 3 - 3 * upper)

    def w_z(to, source):
        return copy(
            wg.at[core, yi, source], wg.at[core, yi, source],
            ws.at[0, to], wr.at[0, source], dev(to * 4 + yi * 2 + xi),
        )

    def w_y(z):
        return copy(wg.at[core, yi, z], wg.at[core, yi, z], ws.at[1, z], wr.at[1, z], dev(y_peer))

    w_c = [
        copy(wg.at[core, row], wg.at[core, row], ws.at[2, 1 + k], wr.at[2, 1 + k], dev(me, other))
        for k, row in enumerate((yi, 1 - yi))
    ]

    def tap(j):
        dz, at = j
        return dz * 3 + (1, 2 - 2 * xi, 2 * xi)[at]

    def product(j, cells, total=None):
        dz = j[0]
        dx = tap(j) - 3 * dz
        for at in range(0, len(cells), 4):
            four = cells[at : at + 4]
            term = lax.dot_general(
                jnp.concatenate([g3[z, x] for z, x in four], axis=1),
                jnp.concatenate([vp[z + dz, dx + x] for z, x in four], axis=1),
                (((1,), (1,)), ((), ())), preferred_element_type=F32,
            )
            total = term if total is None else total + term
        return total

    def own(j):
        first = (0, xi, 1 - xi)[j[1]]
        cells = [(z, first + k) for z in range(4) for k in range(3)]
        held[j[1] - 1, j[0]] = product(j, cells)

    def grad(j):
        if j[1] == 0:
            total = product(j, [(z, x) for z in range(4) for x in range(4)])
        else:
            last_x = (0, 3 - 3 * xi, 3 * xi)[j[1]]
            total = product(j, [(z, last_x) for z in range(4)], held[j[1] - 1, j[0]])
        for h in range(2):
            blocks = total[:, h * 128 : h * 128 + 128].reshape(3, 4, 2, 2, 8, 128)
            for y in range(2):
                for x in range(2):
                    for dy in range(3):
                        first, second = (x, y) if not y_first(j) else (y, x)
                        part[tap(j), h, first, second, :, dy] = blocks[dy, :, y, x]

    def encode(value, bound):
        t = value.reshape(-1, 8, 128) * ((TOP / REACH) / bound)
        a = t * t
        coded = (a * a * (a * t)).reshape(value.shape)
        ends = [bound] if value.shape[0] % 16 else [bound, bound]
        return jnp.concatenate([coded] + ends, axis=0).astype(BF16)

    def decode(coded, count):
        value = coded.astype(F32).reshape(-1, 8, 128)
        bound = value[count]
        value = value[:count]
        size = jnp.exp2(jnp.log2(jnp.abs(value)) * (1.0 / 7.0)) * (bound * (REACH / TOP))
        return jnp.where(value < 0, -size, size), bound

    def stage_a(j):
        i = tap(j)
        return copy(part.at[i, other], ra.at[i], rs_s.at[0, i], rs_r.at[0, i], dev(me, other))

    def y_first(j):
        return j[0] in Y_FIRST[j[1] > 0]

    def path(j):
        return ((xi, x_peer), (yi, y_peer)) if not y_first(j) else ((yi, y_peer), (xi, x_peer))

    def stage_1(j):
        i = tap(j)
        return copy(e1.at[i], r1.at[i], rs_s.at[1, i], rs_r.at[1, i], dev(path(j)[0][1]))

    def stage_2(j):
        i = tap(j)
        return copy(e2.at[i], r2.at[i], rs_s.at[2, i], rs_r.at[2, i], dev(path(j)[1][1]))

    def stage_3(at):
        return [
            copy(e3.at[at, z_to[k]], r3.at[at, k], zs.at[at, k], zr.at[at, k], dev(z_peer[k]))
            for k in range(3)
        ]

    def last(at):
        block = gs.at[core, :, pl.ds(3 * tap((0, at)), 3)]
        return copy(block, block, ls.at[at], lr.at[at], dev(me, other))

    def after_a(j):
        i = tap(j)
        stage_a(j).wait_recv()
        side = path(j)[0][0]
        away = ra[i, 1 - side] + part[i, core, 1 - side]
        e1[i] = encode(away.reshape(192, 128), most[2])
        stage_1(j).start()
        b1[i] = ra[i, side] + part[i, core, side]

    def after_1(j):
        i = tap(j)
        stage_1(j).wait_recv()
        value, bound = decode(r1[i], 24)
        bound = jnp.maximum(bound, most[2])
        scale[i] = bound
        side = path(j)[1][0]
        value = value.reshape(2, 4, 3, 8, 128)
        b1[i] = b1[i] + value
        e2[i] = encode(b1[i, 1 - side].reshape(96, 128), bound)
        stage_2(j).start()

    def after_2(j):
        i = tap(j)
        stage_2(j).wait_recv()
        side = path(j)[1][0]
        value, bound = decode(r2[i], 12)
        scale[i] = jnp.maximum(bound, scale[i])
        b1[i, side] = b1[i, side] + value.reshape(4, 3, 8, 128)

    def to_line(at):
        taps = [tap((dz, at)) for dz in range(3)]
        side = path((0, at))[1][0]
        bound = jnp.maximum(scale[taps[0]], jnp.maximum(scale[taps[1]], scale[taps[2]]))
        for k, c in enumerate(stage_3(at)):
            rows = jnp.concatenate([b1[i, side, z_to[k]] for i in taps], axis=0)
            e3[at, z_to[k]] = encode(rows.reshape(72, 128), bound)
            c.start()

    def from_line(at):
        taps = [tap((dz, at)) for dz in range(3)]
        side = path((0, at))[1][0]
        total = jnp.concatenate([b1[i, side, zi] for i in taps], axis=0)
        for k, c in enumerate(stage_3(at)):
            c.wait_recv()
            total = total + decode(r3[at, k], 9)[0]
        gs[core, :, pl.ds(3 * taps[0], 3)] = total.reshape(3, 3, 8, 128)
        last(at).start()

    def arrange(row):
        for h in range(2):
            for z in range(4):
                pair = [wg[h, row, z, x].astype(F32).reshape(27, 8, 128) for x in range(2)]
                rows = jnp.concatenate(pair, axis=1).astype(BF16).reshape(9, 3, 16, 128)
                for dy in range(3):
                    at = dy * 64 + z * 16
                    w9[row, :, at : at + 16, h * 128 : h * 128 + 128] = rows[:, dy]

    def forward(row, u):
        z, half = u // 2, u % 2
        total = None
        for dz in range(3):
            for dx in range(3):
                at = dx + 2 * half
                cells = jnp.concatenate([vp[z + dz, at], vp[z + dz, at + 1]], axis=1)
                term = jnp.dot(w9[row, dz * 3 + dx], cells, preferred_element_type=F32)
                total = term if total is None else total + term
        edge = lane[0:64]
        for x in range(2):
            cols = slice(x * 128, x * 128 + 128)
            low = jnp.where(edge == 0, 0.0, pltpu.roll(total[0:64, cols], 1, 1))
            high = jnp.where(edge == 127, 0.0, pltpu.roll(total[128:192, cols], 127, 1))
            value = low + total[64:128, cols] + high + bias[:, row].reshape(64, 128)
            for part_z in range(4):
                at = (part_z * 32 + row * 16) * 16 + 4 * z + x + 2 * half
                wide[pl.ds(at, 16, stride=16), :] = value[part_z * 16 : part_z * 16 + 16]

    edge_slot = 4 - 3 * core
    near_corner = copy(vp.at[edge_slot, near_slot], vp.at[send_slot, near_slot], hs.at[3], hr.at[3], dev(me, other))
    far_corner = copy(vp.at[edge_slot, far_slot], vp.at[send_slot, far_slot], hs.at[4], hr.at[4], dev(me, other))

    def near_edge():
        near[0].wait_recv()
        near_corner.start()

    def near_rim():
        near[1].wait_recv()
        near_corner.wait_recv()

    def far_edge():
        @pl.when(has_far)
        def _():
            far[0].wait_recv()
            far_corner.start()

    def far_rim():
        @pl.when(has_far)
        def _():
            far[1].wait_recv()
            far_corner.wait_recv()

    def chunk(j):
        grad(j)
        stage_a(j).start()

    def spread(k):
        z = turns[k]
        w_z(z, z).wait_recv()
        w_y(z).start()

    mid, near_1, far_1 = [[(dz, at) for dz in (1, 0, 2)] for at in (0, 1, 2)]
    inner.wait_recv()
    chunk(mid[0])
    share.wait_recv()
    most[2] = jnp.maximum(most[0], most[1])
    w_x.wait_recv()
    w_y(zi).start()
    for z in turns:
        w_z(z, zi).start()
    chunk(mid[1])
    after_a(mid[0])
    chunk(mid[2])
    after_a(mid[1])
    far_edge()
    after_a(mid[2])
    for j in far_1:
        own(j)
    spread(0)
    far_rim()
    for j in far_1:
        chunk(j)
    after_1(mid[0])
    after_1(mid[1])
    after_a(far_1[0])
    after_a(far_1[1])
    after_1(mid[2])
    after_a(far_1[2])
    near_edge()
    for j in near_1:
        own(j)
    spread(1)
    near_rim()
    for j in near_1:
        chunk(j)
    after_2(mid[0])
    for j in near_1:
        after_a(j)
    spread(2)
    w_c[0].start()
    after_1(near_1[0])
    after_2(mid[1])
    after_1(near_1[1])
    after_2(mid[2])
    to_line(0)
    after_1(near_1[2])
    w_c[0].wait_recv()
    arrange(yi)
    after_1(far_1[0])
    forward(yi, 0)
    after_1(far_1[1])
    forward(yi, 1)
    after_1(far_1[2])
    for z in range(4):
        w_y(z).wait_recv()
    w_c[1].start()
    after_2(near_1[0])
    forward(yi, 2)
    after_2(near_1[1])
    forward(yi, 3)
    after_2(near_1[2])
    to_line(1)
    forward(yi, 4)
    after_2(far_1[0])
    after_2(far_1[1])
    after_2(far_1[2])
    to_line(2)
    forward(yi, 5)
    forward(yi, 6)
    forward(yi, 7)
    w_c[1].wait_recv()
    arrange(1 - yi)
    from_line(0)
    for u in range(4):
        forward(1 - yi, u)
    from_line(1)
    forward(1 - yi, 4)
    forward(1 - yi, 5)
    from_line(2)
    forward(1 - yi, 6)
    forward(1 - yi, 7)
    out_ref[...] = wide[...].astype(BF16)
    for c in near:
        c.wait_send()
    near_corner.wait_send()
    share.wait_send()

    @pl.when(has_far)
    def _():
        for c in far:
            c.wait_send()
        far_corner.wait_send()

    inner.wait_send()
    for z in turns:
        w_z(z, zi).wait_send()
    for c in [w_y(z) for z in range(4)] + w_c + [w_x]:
        c.wait_send()
    for j in mid + near_1 + far_1:
        stage_a(j).wait_send()
        stage_1(j).wait_send()
        stage_2(j).wait_send()
    for at in range(3):
        for c in stage_3(at):
            c.wait_send()
        last(at).wait()
    for h in range(2):
        gw_ref[:, :, h * 128 : h * 128 + 128] = gs[h].reshape(27, 8, 128)


def fused_body(volume, weights, bias, grad_out):
    v = volume.reshape(4096, 128)
    g = grad_out.reshape(2048, 128)
    w = weights.transpose(1, 0, 2).reshape(216, 256)
    b = bias.reshape(1, 128)
    vmem = pl.BlockSpec(memory_space=pltpu.VMEM)
    hold = lambda a: pltpu.with_memory_space_constraint(a, pltpu.HBM)
    hbm = pl.BlockSpec(memory_space=pltpu.HBM)
    dma = pltpu.SemaphoreType.DMA
    out, gw = pl.pallas_call(
        fused_kernel,
        out_shape=(
            jax.ShapeDtypeStruct((2048, 128), BF16),
            jax.ShapeDtypeStruct((27, 8, 256), F32),
        ),
        in_specs=[hbm] * 4,
        out_specs=(vmem, vmem),
        scratch_shapes=[
            pltpu.VMEM((6, 6, 256, 128), BF16),
            pltpu.VMEM((4, 4, 384, 128), BF16),
            pltpu.VMEM((2, 2, 4, 2, 216, 128), BF16),
            pltpu.VMEM((2, 9, 192, 256), BF16),
            pltpu.VMEM((9, 2, 2, 2, 4, 3, 8, 128), F32),
            pltpu.VMEM((9, 2, 2, 4, 3, 8, 128), F32),
            pltpu.VMEM((9, 208, 128), BF16),
            pltpu.VMEM((9, 208, 128), BF16),
            pltpu.VMEM((9, 2, 4, 3, 8, 128), F32),
            pltpu.VMEM((9, 112, 128), BF16),
            pltpu.VMEM((9, 112, 128), BF16),
            pltpu.VMEM((3, 4, 80, 128), BF16),
            pltpu.VMEM((3, 3, 80, 128), BF16),
            pltpu.VMEM((2, 3, 9, 8, 128), F32),
            pltpu.VMEM((3, 8, 128), F32),
            pltpu.VMEM((9, 8, 128), F32),
            dma((8,)), dma((8,)), dma((3, 4)), dma((3, 4)),
            dma((3, 9)), dma((3, 9)), dma((3, 3)), dma((3, 3)),
            dma, dma,
            pltpu.VMEM((4, 2, 16, 128), F32),
            pltpu.VMEM((2048, 128), F32),
            pltpu.VMEM((4096, 128), BF16),
            pltpu.VMEM((2048, 128), BF16),
            pltpu.VMEM((1, 128), F32),
            pltpu.VMEM((4096, 128), F32),
            dma((4,)),
            pltpu.VMEM((2, 3, 384, 256), F32),
            dma((3,)), dma((3,)),
        ],
        compiler_params=pltpu.CompilerParams(
            collective_id=0, has_side_effects=True, vmem_limit_bytes=48 << 20
        ),
    )(hold(v), hold(w), hold(b), hold(g))
    output = out.reshape(128, 4, 4, 128)
    grad_w = gw.transpose(1, 0, 2)
    return (output, grad_w)


def solution(mesh):
    in_specs = (
        P(None, "depth", "filt", None),
        P("filt", None, None),
        P(),
        P(None, "depth", "filt", None),
    )
    out_specs = (P(None, "depth", "filt", None), P("filt", None, None))
    small = mesh.shape["filt"] == 16 and mesh.shape["depth"] == 2

    def body(volume, weights, bias, grad_out):
        shapes = (volume.shape, weights.shape, grad_out.shape)
        if small and shapes == ((256, 4, 4, 128), (8, 27, 256), (128, 4, 4, 128)):
            return fused_body(volume, weights, bias, grad_out)
        return general_body(volume, weights, bias, grad_out)

    return jax.shard_map(body, mesh=mesh, in_specs=in_specs, out_specs=out_specs, check_vma=False)
```
